32 devices in a mesh: rows: 8 (over z, core), seq: 4 (over y, x).
Axes of the slice: x: 2, y: 2, z: 4, core: 2. Of those that a mesh axis runs over, the one named last changes fastest.
Arguments:
- byte_ids: int32 [64, 2048], P('rows', 'seq'), may hold values from 0 to 255
- segment_ids: int32 [64, 2048], P('rows', 'seq'), may hold values from 0 to 7, never falling along the last dimension, each value on 1 to 1024 neighbouring positions
- table: bfloat16 [256, 768], replicated, may hold values from -6 to 6
- conv_weight: bfloat16 [4, 768], replicated, may hold values from -3 to 3
- scorer: bfloat16 [768], replicated, may hold values from -0.4375 to 0.4375
- cotangent: bfloat16 [64, 1024, 768], P('rows', 'seq'), may hold values from -6 to 6
Outputs:
- blocks_out: bfloat16 [64, 1024, 768], P('rows', 'seq')
- table_grad: float32 [256, 768], P('seq')
- conv_grad: float32 [4, 768], replicated
- scorer_grad: float32 [768], replicated
The draws below stay inside these ranges and needn't reach their ends.
Inputs may be any that keep to these rules, and one draw needn't show every extreme that they name: `segment_ids`: within each row the numbers never fall; a document spans at most 1024 bytes and may cross from one piece of the row to the next.
All inputs are finite; a program needn't handle non-finite values.
Results may differ from the reference program's by a relative error of at most 0.001.
Values sent between devices are 32-bit elements; how exact they have to be, the bound alone decides.
No kernel may reach another device: no remote copies, remote signals or barrier semaphores. Data moves between devices by JAX's collectives and lax.ppermute only.
A program may use at most 320 MiB of HBM per device.

```python
import math
import jax
import jax.numpy as jnp
import numpy as np
from jax import lax

D = 768
VOCAB = 256
KERNEL = 4
BLOCKS = 4
LENGTH = 2048
ROWS = 64


def place_ends(values, rng, smallest, high):
    extent = values.shape
    index_at = [jax.random.randint(jax.random.fold_in(rng, axis), (), 0, extent[axis]) for axis in range(len(extent))]
    values = values.at[tuple(index_at)].set(smallest)
    longest = extent.index(max(extent))
    index_at[longest] = (index_at[longest] + 1) % extent[longest]
    return values.at[tuple(index_at)].set(high)


def level_of(key, shape, split, least, top_value):
    level = 1.0
    for axis_at, shards_of in split:
        heights = jax.random.uniform(jax.random.fold_in(jax.random.fold_in(key, 6), axis_at), (shards_of,), jnp.float32, least / len(split), top_value / len(split))
        level = level * jnp.repeat(jnp.exp(heights), shape[axis_at] // shards_of).reshape((-1,) + (1,) * (len(shape) - 1 - axis_at))
    return level


def rank_table(number_of, slope):
    portions = [(1 << 20) // math.isqrt(grade ** slope) + 1 for grade in range(1, number_of + 1)]
    deviation = 1 + sum(portions) // (1 << 30)
    return np.cumsum(np.array([max(1, weight // deviation) for weight in portions]))


def ranked(own_key, extent, count, lean):
    listing = rank_table(count, lean)
    ticket = jax.random.randint(jax.random.fold_in(own_key, 1), extent, 0, int(listing[count - 1]))
    grade = jnp.searchsorted(jnp.asarray(listing, jnp.int32), ticket, side="right")
    return jax.random.permutation(jax.random.fold_in(own_key, 2), count)[grade].astype(jnp.int32)


def length_profile(count, total, reach, slope):
    loads = [(1 << 20) // math.isqrt(standing ** slope) + 1 for standing in range(2, count + 1)]
    spare, holding = total - reach - (count - 1), [1] * (count - 1)
    while spare > 0:
        movable = [i for i in range(count - 1) if holding[i] < reach]
        whole, budget = sum([loads[i] for i in movable]), spare
        for i in movable:
            extra = min(reach - holding[i], max(1, budget * loads[i] // whole), spare)
            holding[i] = holding[i] + extra
            spare = spare - extra
    return np.array([reach] + holding)


def uneven(stream_key, amount, total, reach, slope):
    if amount == 2:
        one = jax.random.randint(stream_key, (), max(1, total - reach), min(reach, total - 1) + 1)
        return jnp.stack([one, total - one])
    sizes = jnp.asarray(length_profile(amount, total, reach, slope), jnp.int32)
    pairs = (amount - 1) // 2
    donor, sink = sizes[1:1 + 2 * pairs:2], sizes[2:2 + 2 * pairs:2]
    margin = jnp.minimum(donor - 1, reach - sink)
    moved = jax.random.randint(jax.random.fold_in(stream_key, 1), (pairs,), 0, 1 << 20) % (margin + 1)
    sizes = sizes.at[1:1 + 2 * pairs:2].set(donor - moved).at[2:2 + 2 * pairs:2].set(sink + moved)
    return sizes[jax.random.permutation(jax.random.fold_in(stream_key, 2), amount)]


def normal_values(rng, dims, spread, most, split=(), held_as=jnp.bfloat16):
    drawn = jax.random.normal(rng, dims, jnp.float32) * spread
    if len(split) > 0:
        drawn = level_of(rng, dims, split, -0.22, 0.18) * drawn
    return jnp.clip(drawn, min=-most, max=most).astype(held_as)


def setup_inputs(seed: int = 0) -> dict:
    splits = jax.random.split(jax.random.key(seed), 7)
    return {
        "byte_ids": place_ends(ranked(splits[0], (ROWS, LENGTH), VOCAB, 2), jax.random.fold_in(splits[0], 3), 0, VOCAB - 1).astype(jnp.int32),
        "segment_ids": jax.vmap(lambda own: jnp.searchsorted(jnp.cumsum(uneven(own, max(4, LENGTH // 256), LENGTH, LENGTH // 2, 1)), jnp.arange(LENGTH), side="right"))(jax.random.split(splits[1], ROWS)).reshape((ROWS, LENGTH)).astype(jnp.int32),
        "table": normal_values(splits[2], (VOCAB, D), 1.0, 6.0),
        "conv_weight": normal_values(splits[3], (KERNEL, D), 0.5, 3.0),
        "scorer": normal_values(splits[4], (D,), (D // 4) ** -0.5, 0.4375),
        "cotangent": normal_values(splits[5], (ROWS, LENGTH // 2, D), 1.0, 6.0, ((0, 8), (1, 4))),
    }


@jax.custom_vjp
def low(v):
    return lax.optimization_barrier(v.astype(jnp.bfloat16)).astype(jnp.float32)

@jax.custom_vjp
def low_back(v):
    return v

def low_keep(v):
    return (low(v), None)

def low_pass(kept, grad):
    return (grad,)

def back_keep(v):
    return (v, None)

def back_low(kept, grad):
    return (low(grad),)
low.defvjp(low_keep, low_pass)
low_back.defvjp(back_keep, back_low)

def shifted(value, offset, filler):
    if offset == 0:
        return value
    widths = [(offset, 0)] + [(0, 0)] * (value.ndim - 1)
    padded = jnp.pad(value, widths, constant_values=filler)
    return padded[:value.shape[0]]

def forward_row(table32, weights32, scorer32, byte_row, seg_row):
    embedded = table32[byte_row]
    masks = [(shifted(seg_row, offset, -1) == seg_row).astype(jnp.float32) for offset in range(4)]
    conved = jnp.zeros_like(embedded)
    for offset in range(KERNEL):
        conved = conved + weights32[offset] * shifted(embedded, offset, 0.0) * masks[offset][:, None]
    running = jnp.zeros_like(embedded)
    counted = jnp.zeros(seg_row.shape, jnp.float32)
    pooled = []
    for offset in range(BLOCKS):
        running = running + masks[offset][:, None] * shifted(conved, offset, 0.0)
        counted = counted + masks[offset]
        pooled.append(running / counted[:, None])
    scores = jnp.stack([jnp.dot(level, scorer32, precision=lax.Precision.HIGHEST) for level in pooled])
    probs = jax.nn.softmax(scores, axis=0)
    mixed = sum((probs[level][:, None] * pooled[level] for level in range(BLOCKS)))
    return lax.optimization_barrier(jnp.mean(mixed.reshape(mixed.shape[0] // 2, 2, mixed.shape[1]), axis=1))

def reference(byte_ids, segment_ids, table, conv_weight, scorer, cotangent):
    table32 = table.astype(jnp.float32)
    weights32 = conv_weight.astype(jnp.float32)
    scorer32 = scorer.astype(jnp.float32)

    def one_row(totals, items):
        byte_row, seg_row, upstream = items

        def run(tab, wts, scr):
            return forward_row(tab, wts, scr, byte_row, seg_row)
        result, pullback = jax.vjp(run, table32, weights32, scorer32)
        grads = pullback(upstream.astype(jnp.float32))
        totals = (totals[0] + grads[0], totals[1] + grads[1], totals[2] + grads[2])
        return (totals, result.astype(jnp.bfloat16))
    start = (jnp.zeros(table32.shape, jnp.float32), jnp.zeros(weights32.shape, jnp.float32), jnp.zeros(scorer32.shape, jnp.float32))
    totals, blocks_out = lax.scan(one_row, start, (byte_ids, segment_ids, cotangent))
    return (blocks_out, totals[0], totals[1], totals[2])
```

```python
import functools

import jax
import jax.numpy as jnp
from jax import lax
from jax.experimental import pallas as pl
from jax.experimental.pallas import tpu as pltpu
from jax.sharding import PartitionSpec as P

TAPS = 4
REACH = 5
SPAN = 8
LANES = 128
F32 = jnp.float32
BF16 = jnp.bfloat16
NT = (((1,), (1,)), ((), ()))


def split(x):
    hi = x.astype(BF16)
    return hi, (x - hi.astype(F32)).astype(BF16)


def dot(a, b):
    return jnp.dot(a, b, preferred_element_type=F32)


def dot_nt(a, b):
    return lax.dot_general(a, b, NT, preferred_element_type=F32)


def lanes_of(width):
    step = min(width, LANES)
    return [pl.ds(at, step) for at in range(0, width, step)]


def response_kernel(table_ref, weight_ref, scorer_ref, cot_ref, resp_ref, score_ref, table_t_ref, weight_b_ref, taps):
    vocab, width = table_ref.shape

    @pl.when(pl.program_id(0) == 0)
    def _():
        table = table_ref[...].astype(F32)
        weight = weight_ref[...].astype(F32)
        for k in range(TAPS):
            hi, lo = split(weight[k : k + 1] * table)
            taps[pl.ds(k * vocab, vocab), pl.ds(0, width)] = hi
            taps[pl.ds(k * vocab, vocab), pl.ds(width, width)] = lo
            weight_b_ref[k] = jnp.transpose(jnp.broadcast_to(weight[k : k + 1], (LANES, width)))
        hi, lo = split(weight * scorer_ref[...].astype(F32))
        score_ref[...] = dot_nt(hi, table_ref[...]) + dot_nt(lo, table_ref[...])
        table_t_ref[...] = jnp.transpose(table).astype(BF16)

    cot = cot_ref[0]
    resp_ref[0] = dot_nt(taps[...], jnp.concatenate([cot, cot], axis=1))


def response(table, conv_weight, scorer, cotangent):
    rows, pairs, width = cotangent.shape
    vocab = table.shape[0]
    whole = lambda shape: pl.BlockSpec(shape, lambda i: (0,) * len(shape))
    return pl.pallas_call(
        response_kernel,
        grid=(rows,),
        in_specs=[
            whole((vocab, width)),
            whole((TAPS, width)),
            whole((1, width)),
            pl.BlockSpec((1, pairs, width), lambda i: (i, 0, 0)),
        ],
        out_specs=[
            pl.BlockSpec((1, TAPS * vocab, pairs), lambda i: (i, 0, 0)),
            whole((TAPS, vocab)),
            whole((width, vocab)),
            whole((TAPS, width, LANES)),
        ],
        out_shape=[
            jax.ShapeDtypeStruct((rows, TAPS * vocab, pairs), F32),
            jax.ShapeDtypeStruct((TAPS, vocab), F32),
            jax.ShapeDtypeStruct((width, vocab), BF16),
            jax.ShapeDtypeStruct((TAPS, width, LANES), F32),
        ],
        scratch_shapes=[pltpu.VMEM((TAPS * vocab, 2 * width), BF16)],
        name="response",
    )(table, conv_weight, scorer[None], cotangent)


def look_up(rows_of, index):
    parts = []
    for at in range(0, index.shape[1], LANES):
        part = index[:, at : at + LANES]
        low = part & (LANES - 1)
        take = lambda h: jnp.take_along_axis(
            jnp.broadcast_to(rows_of[h], part.shape), low, axis=1, mode="promise_in_bounds"
        )
        parts.append(jnp.where(part < LANES, take(0), take(1)))
    return jnp.concatenate(parts, axis=1) if len(parts) > 1 else parts[0]


def gradient_kernel(
    code_ref, table_ref, weight_ref, scorer_ref, score_ref, cot_ref, resp_ref,
    mix_ref, table_grad_ref, rest_ref,
    byte_scr, pick_scr, seg_scr, prob_scr, gam_scr, look_scr, eta_scr, sum_scr,
):
    rows, padded = byte_scr.shape[1:]
    vocab, width = table_ref.shape
    pairs = cot_ref.shape[1]
    row = pl.program_id(0)
    tiles = lanes_of(pairs)

    def same(r, k):
        return jnp.where(seg_scr[r] == seg_scr[r + k], 1.0, 0.0)

    def counts(start):
        keep = [same(start, k) for k in range(TAPS)]
        total, inverse = keep[0], []
        for b in range(TAPS):
            if b:
                total = total + keep[b]
            inverse.append(1.0 / total)
        return keep, inverse

    @pl.when(row == 0)
    def _():
        codes = code_ref[...].astype(F32).astype(BF16)
        reach = codes.shape[1]
        halo = reach - 2 * pairs
        at = lax.broadcasted_iota(jnp.int32, (reach, padded), 0)
        pair = lax.broadcasted_iota(jnp.int32, (reach, padded), 1)
        shift = at - 2 * pair - (halo + 1)
        for s in range(SPAN):
            pick = jnp.where(shift == -s, 1.0, 0.0).astype(BF16)
            found = dot(codes, pick)
            byte_scr[s] = found[:rows].astype(jnp.int32)
            seg_scr[s] = found[rows:]
        scored = []
        tables = [[score_ref[k : k + 1, h * LANES : (h + 1) * LANES] for h in range(2)] for k in range(TAPS)]
        for r in range(REACH):
            scored.append(sum(same(r, k) * look_up(tables[k], byte_scr[r + k]) for k in range(TAPS)))
        beta = [0.0] * REACH
        for start in range(2):
            keep, inverse = counts(start)
            running, level = 0.0, []
            for b in range(TAPS):
                running = running + keep[b] * scored[start + b]
                level.append(running * inverse[b])
            top = functools.reduce(jnp.maximum, level)
            level = [jnp.exp(x - top) for x in level]
            norm = 1.0 / sum(level)
            level = [x * norm for x in level]
            share = 0.0
            for b in range(TAPS - 1, -1, -1):
                prob_scr[start * TAPS + b] = level[b]
                share = share + level[b] * inverse[b]
                beta[start + b] = beta[start + b] + 0.5 * keep[b] * share
        for r in range(REACH):
            for k in range(TAPS):
                gam = beta[r] * same(r, k)
                for i in range(rows):
                    gam_scr[i, pl.ds(r * TAPS + k, 1)] = gam[i : i + 1]
        for s in range(SPAN):
            for i in range(rows):
                pick_scr[i, pl.ds(s, 1)] = byte_scr[s, i : i + 1]

    for lane in tiles:
        size = lane.size
        byte = [pick_scr[row, pl.ds(s, 1), lane] for s in range(SPAN)]
        base = lax.broadcasted_iota(jnp.int32, (8, size), 0)
        found = [[jnp.zeros((8, size), F32) for _ in range(TAPS)] for _ in range(REACH)]
        for v in range(0, vocab, 8):
            hit = [b == base + v for b in byte]
            for k in range(TAPS):
                value = resp_ref[0, pl.ds(k * vocab + v, 8), lane]
                for r in range(REACH):
                    found[r][k] = jnp.where(hit[r + k], value, found[r][k])
        for r in range(REACH):
            for k in range(TAPS):
                look_scr[row, pl.ds(r * TAPS + k, 1), lane] = jnp.sum(found[r][k], axis=0, keepdims=True)
    for lane in tiles:
        size = lane.size
        byte = [pick_scr[row, pl.ds(s, 1), lane] for s in range(SPAN)]
        gam = [gam_scr[row, pl.ds(q, 1), lane] for q in range(REACH * TAPS)]
        base = lax.broadcasted_iota(jnp.int32, (16, size), 0)
        for v in range(0, vocab, 16):
            hit = [b == base + v for b in byte]
            for k in range(TAPS):
                mixed = sum(jnp.where(hit[r + k], gam[r * TAPS + k], 0.0) for r in range(REACH))
                hi, lo = split(mixed)
                mix_ref[0, k, pl.ds(v, 16), lane] = hi
                mix_ref[0, k, pl.ds(vocab + v, 16), lane] = lo
    cot = cot_ref[0]
    for k in range(TAPS):
        hi, lo = mix_ref[0, k, :vocab], mix_ref[0, k, vocab:]
        if pairs % LANES == 0:
            part = dot(jnp.concatenate([hi, lo], axis=1), jnp.concatenate([cot, cot], axis=0))
        else:
            part = dot(hi, cot) + dot(lo, cot)
        where = pl.ds(k * vocab, vocab)

        @pl.when(row == 0)
        def _():
            sum_scr[where] = part

        @pl.when(row > 0)
        def _():
            sum_scr[where] += part

    @pl.when(row == rows - 1)
    def _():
        eta = [0.0] * REACH
        products = [sum(same(r, k) * look_scr[:, r * TAPS + k] for k in range(TAPS)) for r in range(REACH)]
        for start in range(2):
            keep, inverse = counts(start)
            prob = [prob_scr[start * TAPS + b] for b in range(TAPS)]
            running, grad = 0.0, []
            for b in range(TAPS):
                running = running + keep[b] * products[start + b]
                grad.append(0.5 * running * inverse[b])
            mean = sum(p * g for p, g in zip(prob, grad))
            share = 0.0
            for b in range(TAPS - 1, -1, -1):
                share = share + prob[b] * (grad[b] - mean) * inverse[b]
                eta[start + b] = eta[start + b] + keep[b] * share
        eta_scr[...] = jnp.zeros_like(eta_scr)
        for r in range(REACH):
            for k in range(TAPS):
                value = eta[r] * same(r, k)
                hi = value.astype(BF16).astype(F32)
                lo = value - hi
                for i in range(rows):
                    eta_scr[i, r + k, k : k + 1] = hi[i : i + 1]
                    eta_scr[i, r + k, TAPS + k : TAPS + k + 1] = lo[i : i + 1]
        base = lax.broadcasted_iota(jnp.int32, (vocab, pairs), 0)

        def scatter(i, total):
            for s in range(SPAN):
                hot = jnp.where(pick_scr[i, pl.ds(s, 1), pl.ds(0, pairs)] == base, 1.0, 0.0).astype(BF16)
                total = total + dot_nt(hot, eta_scr[i, s, :, pl.ds(0, pairs)].astype(BF16))
            return total

        spread = lax.fori_loop(0, rows, scatter, jnp.zeros((vocab, 2 * TAPS), F32))
        spread = spread[:, :TAPS] + spread[:, TAPS:]
        table = table_ref[...].astype(F32)
        weight = weight_ref[...].astype(F32)
        scorer = scorer_ref[...].astype(F32)
        grad, score_grad, conv = 0.0, 0.0, []
        for k in range(TAPS):
            column = spread[:, k : k + 1]
            total = sum_scr[pl.ds(k * vocab, vocab)] + column * scorer
            grad = grad + weight[k : k + 1] * total
            conv.append(jnp.sum(table * total, axis=0, keepdims=True))
            score_grad = score_grad + weight[k : k + 1] * jnp.sum(table * column, axis=0, keepdims=True)
        table_grad_ref[...] = grad
        rest_ref[...] = jnp.concatenate(conv + [score_grad, jnp.zeros((8 - TAPS - 1, width), F32)], axis=0)


def gradient(codes, table, conv_weight, scorer, scores, cotangent, resp):
    rows, pairs, width = cotangent.shape
    vocab = table.shape[0]
    padded = -(-pairs // LANES) * LANES
    whole = lambda shape: pl.BlockSpec(shape, lambda i: (0,) * len(shape))
    return pl.pallas_call(
        gradient_kernel,
        grid=(rows,),
        in_specs=[
            whole(codes.shape),
            whole((vocab, width)),
            whole((TAPS, width)),
            whole((1, width)),
            whole((TAPS, vocab)),
            pl.BlockSpec((1, pairs, width), lambda i: (i, 0, 0)),
            pl.BlockSpec((1, TAPS * vocab, pairs), lambda i: (i, 0, 0)),
        ],
        out_specs=[
            pl.BlockSpec((1, TAPS, 2 * vocab, pairs), lambda i: (i, 0, 0, 0)),
            whole((vocab, width)),
            whole((8, width)),
        ],
        out_shape=[
            jax.ShapeDtypeStruct((rows, TAPS, 2 * vocab, pairs), BF16),
            jax.ShapeDtypeStruct((vocab, width), F32),
            jax.ShapeDtypeStruct((8, width), F32),
        ],
        scratch_shapes=[
            pltpu.VMEM((SPAN, rows, padded), jnp.int32),
            pltpu.VMEM((rows, SPAN, padded), jnp.int32),
            pltpu.VMEM((SPAN, rows, padded), F32),
            pltpu.VMEM((2 * TAPS, rows, padded), F32),
            pltpu.VMEM((rows, REACH * TAPS, padded), F32),
            pltpu.VMEM((rows, REACH * TAPS, padded), F32),
            pltpu.VMEM((rows, SPAN, 2 * TAPS, padded), F32),
            pltpu.VMEM((TAPS * vocab, width), F32),
        ],
        name="gradient",
    )(codes, table, conv_weight, scorer[None], scores, cotangent, resp)


def blocks_kernel(table_t_ref, weight_b_ref, mix_ref, out_ref):
    width = table_t_ref.shape[0]
    pairs = out_ref.shape[1]
    step = 256
    for d in range(0, width, step):
        table_t = table_t_ref[pl.ds(d, step)]
        both = jnp.concatenate([table_t, table_t], axis=1)
        total = 0.0
        for k in range(TAPS):
            weight = weight_b_ref[k, pl.ds(d, step)]
            if pairs > LANES:
                weight = jnp.concatenate([weight] * (pairs // LANES), axis=1)
            else:
                weight = weight[:, :pairs]
            total = total + weight * dot(both, mix_ref[0, k])
        out_ref[0, :, pl.ds(d, step)] = jnp.transpose(total).astype(BF16)


def blocks(table_t, weight_b, mix):
    rows, _, _, pairs = mix.shape
    width, vocab = table_t.shape
    whole = lambda shape: pl.BlockSpec(shape, lambda i: (0,) * len(shape))
    return pl.pallas_call(
        blocks_kernel,
        grid=(rows,),
        in_specs=[
            whole((width, vocab)),
            whole(weight_b.shape),
            pl.BlockSpec((1,) + mix.shape[1:], lambda i: (i, 0, 0, 0)),
        ],
        out_specs=pl.BlockSpec((1, pairs, width), lambda i: (i, 0, 0)),
        out_shape=jax.ShapeDtypeStruct((rows, pairs, width), BF16),
        name="blocks",
    )(table_t, weight_b, mix)


def reduce_all(table_grad, rest, rows_axis, seq_axis):
    ranks, parts = lax.axis_size(rows_axis), lax.axis_size(seq_axis)
    rank, part = lax.axis_index(rows_axis), lax.axis_index(seq_axis)

    def swap(x, axis, stride):
        return lax.ppermute(x, axis, [(i, i ^ stride) for i in range(lax.axis_size(axis))])

    vocab, width = table_grad.shape
    half = width // 2
    core = rank % 2
    whole = jnp.concatenate([table_grad, rest], axis=0)
    mine = lax.dynamic_slice_in_dim(whole, core * half, half, 1)
    other = lax.dynamic_slice_in_dim(whole, (1 - core) * half, half, 1)
    mine = mine + swap(other, rows_axis, 1)
    grad, rest = mine[:vocab], mine[vocab:]
    stride = parts // 2
    while stride:
        size = grad.shape[0] // 2
        bit = (part // stride) % 2
        sent = jnp.concatenate([lax.dynamic_slice_in_dim(grad, (1 - bit) * size, size, 0), rest], axis=0)
        kept = jnp.concatenate([lax.dynamic_slice_in_dim(grad, bit * size, size, 0), rest], axis=0)
        got = kept + swap(sent, seq_axis, stride)
        grad, rest = got[:size], got[size:]
        stride //= 2
    mine = jnp.concatenate([grad, rest], axis=0)
    stride = 2
    while stride < ranks:
        mine = mine + swap(mine, rows_axis, stride)
        stride *= 2
    other = swap(mine, rows_axis, 1)
    both = jnp.where(
        core == 0, jnp.concatenate([mine, other], axis=1), jnp.concatenate([other, mine], axis=1)
    )
    share = vocab // parts
    return both[:share], both[share : share + TAPS], both[share + TAPS]


def per_device(byte_ids, segment_ids, table, conv_weight, scorer, cotangent):
    parts = lax.axis_size("seq")
    codes = jnp.concatenate([byte_ids, segment_ids], axis=0)
    tail = codes[:, -LANES:]
    halo = lax.ppermute(tail, "seq", [(i, i + 1) for i in range(parts - 1)])
    halo = jnp.where(lax.axis_index("seq") == 0, -1, halo)
    resp, scores, table_t, weight_b = response(table, conv_weight, scorer, cotangent)
    codes = jnp.concatenate([halo, codes], axis=1)
    mix, table_grad, rest = gradient(codes, table, conv_weight, scorer, scores, cotangent, resp)
    blocks_out = blocks(table_t, weight_b, mix)
    table_grad, conv_grad, scorer_grad = reduce_all(table_grad, rest, "rows", "seq")
    return (blocks_out, table_grad, conv_grad, scorer_grad)


def solution(mesh):
    return jax.shard_map(
        per_device,
        mesh=mesh,
        in_specs=(P("rows", "seq"), P("rows", "seq"), P(), P(), P(), P("rows", "seq", None)),
        out_specs=(P("rows", "seq", None), P("seq", None), P(), P()),
        check_vma=False,
    )
```

```python
import functools

import jax
import jax.numpy as jnp
from jax import lax
from jax.experimental import pallas as pl
from jax.experimental.pallas import tpu as pltpu
from jax.sharding import PartitionSpec as P

TAPS = 4
REACH = 5
SPAN = 8
LANES = 128
F32 = jnp.float32
BF16 = jnp.bfloat16
NT = (((1,), (1,)), ((), ()))


def split(x):
    hi = x.astype(BF16)
    return hi, (x - hi.astype(F32)).astype(BF16)


def dot(a, b):
    return jnp.dot(a, b, preferred_element_type=F32)


def dot_nt(a, b):
    return lax.dot_general(a, b, NT, preferred_element_type=F32)


def lanes_of(width):
    step = min(width, LANES)
    return [pl.ds(at, step) for at in range(0, width, step)]


def score_kernel(table_ref, weight_ref, scorer_ref, score_ref):
    hi, lo = split(weight_ref[...].astype(F32) * scorer_ref[...].astype(F32))
    score_ref[...] = dot_nt(hi, table_ref[...]) + dot_nt(lo, table_ref[...])


def score_table(table, conv_weight, scorer):
    return pl.pallas_call(
        score_kernel,
        out_shape=jax.ShapeDtypeStruct((TAPS, table.shape[0]), F32),
        name="score_table",
    )(table, conv_weight, scorer[None])


def look_up(rows_of, index):
    parts = []
    for at in range(0, index.shape[1], LANES):
        part = index[:, at : at + LANES]
        low = part & (LANES - 1)
        take = lambda h: jnp.take_along_axis(
            jnp.broadcast_to(rows_of[h], part.shape), low, axis=1, mode="promise_in_bounds"
        )
        parts.append(jnp.where(part < LANES, take(0), take(1)))
    return jnp.concatenate(parts, axis=1)


HALO = 16
GROUPS = 4


def main_kernel(
    code_ref, table_ref, weight_ref, scorer_ref, score_ref, cot_ref,
    out_ref, table_grad_ref, rest_ref,
    pick_scr, gam_scr, col_scr, column_scr, keep_scr, prob_scr, rim_scr, emb_a, emb_b, conv_scr, dcol_scr, prod_scr, zeta_scr,
    weight_scr, mix_a, mix_b, sum_scr,
):
    rows, _, padded = pick_scr.shape
    vocab, width = table_ref.shape
    pairs = cot_ref.shape[1]
    row = pl.program_id(0)
    tiles = width // LANES

    def back(x, n):
        return pltpu.roll(x, n % padded, axis=1) if n % padded else x

    def keeps(parity, k):
        return keep_scr[parity * TAPS + k] if k else 1.0

    def same(r, k):
        return back(keep_scr[r % 2 * TAPS + k], r // 2) if k else 1.0

    def counts(start):
        total, inverse = 1.0, [1.0]
        for b in range(1, TAPS):
            total = total + keeps(start, b)
            inverse.append(1.0 / total)
        return inverse

    def put(scr, q, value):
        for i in range(rows):
            scr[i, pl.ds(q, 1)] = value[i : i + 1]

    @pl.when(row == 0)
    def _():
        codes = code_ref[...].astype(F32).astype(BF16)
        reach = codes.shape[1]
        ahead = reach - 2 * pairs
        at = lax.broadcasted_iota(jnp.int32, (reach, padded), 0) - ahead
        lane = lax.broadcasted_iota(jnp.int32, (reach, padded), 1)
        place = at - 2 * jnp.where(lane < pairs, lane, lane - padded)
        byte, seg = [], []
        for parity in range(2):
            found = dot(codes, jnp.where(place == 1 - parity, 1.0, 0.0).astype(BF16))
            byte.append(found[:rows])
            seg.append(found[rows:])
        for parity in range(2):
            put(col_scr, parity, byte[parity])
            for k in range(1, TAPS):
                s = parity + k
                keep = jnp.where(seg[parity] == back(seg[s % 2], s // 2), 1.0, 0.0)
                keep_scr[parity * TAPS + k] = keep
                put(col_scr, 2 + parity * (TAPS - 1) + k - 1, keep)
        byte = [b.astype(jnp.int32) for b in byte]
        for s in range(SPAN):
            put(pick_scr, s, back(byte[s % 2], s // 2))
        found = []
        for k in range(TAPS):
            halves = [score_ref[k : k + 1, h * LANES : (h + 1) * LANES] for h in range(2)]
            found.append([look_up(halves, byte[parity]) for parity in range(2)])
        scored = [
            sum(keeps(parity, k) * back(found[k][(parity + k) % 2], (parity + k) // 2) for k in range(TAPS))
            for parity in range(2)
        ]
        beta = [0.0] * REACH
        for start in range(2):
            inverse = counts(start)
            running, level = 0.0, []
            for b in range(TAPS):
                running = running + keeps(start, b) * back(scored[(start + b) % 2], (start + b) // 2)
                level.append(running * inverse[b])
            top = functools.reduce(jnp.maximum, level)
            level = [jnp.exp(x - top) for x in level]
            norm = 1.0 / sum(level)
            level = [x * norm for x in level]
            share = 0.0
            for b in range(TAPS - 1, -1, -1):
                prob_scr[start * TAPS + b] = level[b]
                share = share + level[b] * inverse[b]
                beta[start + b] = beta[start + b] + 0.5 * keeps(start, b) * share
        for r in range(REACH):
            put(col_scr, 2 * TAPS + r, beta[r])
            for k in range(TAPS):
                put(gam_scr, r * TAPS + k, beta[r] * same(r, k))

    deep = HALO + pairs
    group = pairs // GROUPS
    part_v = vocab // GROUPS

    embs, mixes = (emb_a, emb_b), (mix_a, mix_b)

    def spot(parity, d):
        return (parity * tiles + d) * deep

    def embed(i, slot, j):
        at = pl.multiple_of(HALO + j * group, 8)
        column = column_scr[i, pl.ds(at, group)]
        value = lax.broadcasted_iota(jnp.int32, (group, vocab), 1).astype(F32)
        hot = [jnp.where(column[:, p : p + 1] == value, 1.0, 0.0).astype(BF16) for p in range(2)]
        found = dot(jnp.concatenate(hot, axis=0), table_ref[...])
        for p in range(2):
            for d in range(tiles):
                to = pl.multiple_of(spot(p, d) + at, 8)
                embs[slot][pl.ds(to, group)] = found[p * group : (p + 1) * group, d * LANES : (d + 1) * LANES]

    def embed_rim(i, slot):
        for p in range(2):
            for d in range(tiles):
                to = pl.multiple_of(spot(p, d), 8)
                embs[slot][pl.ds(to, HALO)] = rim_scr[p, d, i]

    def mixing(i, slot, j):
        for lane in lanes_of(pairs):
            size = lane.size
            byte = [pick_scr[i, pl.ds(s, 1), lane] for s in range(SPAN)]
            gam = [gam_scr[i, pl.ds(q, 1), lane] for q in range(REACH * TAPS)]
            base = lax.broadcasted_iota(jnp.int32, (16, size), 0) + j * part_v
            for v in range(0, part_v, 16):
                hit = [b == base + v for b in byte]
                at = pl.ds(pl.multiple_of(j * part_v + v, 16), 16)
                for k in range(TAPS):
                    mixed = sum(jnp.where(hit[r + k], gam[r * TAPS + k], 0.0) for r in range(REACH))
                    hi, lo = split(mixed)
                    mixes[slot][k, 0, at, lane] = hi
                    mixes[slot][k, 1, at, lane] = lo

    def gather(slot, j):
        cot = cot_ref[0]
        at = pl.ds(pl.multiple_of(j * part_v, 16), part_v)
        hi = jnp.concatenate([mixes[slot][k, 0, at] for k in range(TAPS)], axis=0)
        lo = jnp.concatenate([mixes[slot][k, 1, at] for k in range(TAPS)], axis=0)
        if pairs % LANES == 0:
            part = dot(jnp.concatenate([hi, lo], axis=1), jnp.concatenate([cot, cot], axis=0))
        else:
            part = dot(hi, cot) + dot(lo, cot)
        for k in range(TAPS):
            sum_scr[pl.ds(pl.multiple_of(k * vocab + j * part_v, 8), part_v)] += part[k * part_v : (k + 1) * part_v]

    def conved(slot, at, column, d):
        taken = [embs[slot][pl.ds(spot(s % 2, d) + at - s // 2, 8)] for s in range(REACH)]
        for p in range(2):
            total = weight_scr[0, d] * taken[p]
            for k in range(1, TAPS):
                keep = column[:, 2 + p * (TAPS - 1) + k - 1 :][:, :1]
                total = total + keep * (weight_scr[k, d] * taken[p + k])
            conv_scr[pl.ds(pl.multiple_of(spot(p, d) + at, 8), 8)] = total

    lane_at = lax.broadcasted_iota(jnp.int32, (8, LANES), 1) - 8 * row

    def convolve(slot, j):
        for t in range(0, group, 8):
            at = pl.multiple_of(HALO + j * group + t, 8)
            column = column_scr[row, pl.ds(at, 8)]
            for d in range(tiles):
                conved(slot, at, column, d)

    def blocks(j):
        for t in range(0, group, 16):
            start = pl.multiple_of(j * group + t, 16)
            column = [column_scr[row, pl.ds(pl.multiple_of(HALO + start + u, 8), 8)] for u in (0, 8)]
            products = [[0.0] * REACH for _ in range(2)]
            for d in range(tiles):
                lanes = pl.ds(d * LANES, LANES)
                grad = cot_ref[0, pl.ds(start, 16), lanes].astype(F32)
                out = []
                for u in range(2):
                    at = HALO + start + 8 * u
                    mixed = 0.0
                    for r in range(REACH):
                        conv = conv_scr[pl.ds(spot(r % 2, d) + at - r // 2, 8)]
                        products[u][r] = products[u][r] + grad[8 * u : 8 * u + 8] * conv
                        mixed = mixed + column[u][:, 2 * TAPS + r : 2 * TAPS + r + 1] * conv
                    out.append(mixed)
                out_ref[0, pl.ds(start, 16), lanes] = jnp.concatenate(out, axis=0).astype(BF16)
            for u in range(2):
                to = pl.ds(pl.multiple_of(start + 8 * u, 8), 8)
                found = dcol_scr[to]
                for r in range(REACH):
                    found = jnp.where(lane_at == r, jnp.sum(products[u][r], axis=1, keepdims=True), found)
                dcol_scr[to] = found

    @pl.when(row == 0)
    def _():
        for i in range(rows):
            column = jnp.transpose(col_scr[i])
            column_scr[i, pl.ds(0, HALO)] = column[padded - HALO :]
            column_scr[i, pl.ds(HALO, pairs)] = column[:pairs]
        value = lax.broadcasted_iota(jnp.int32, (HALO, vocab), 1).astype(F32)
        for p in range(2):
            hot = [
                jnp.where(column_scr[i, pl.ds(0, HALO)][:, p : p + 1] == value, 1.0, 0.0).astype(BF16)
                for i in range(rows)
            ]
            found = dot(jnp.concatenate(hot, axis=0), table_ref[...])
            for d in range(tiles):
                for i in range(rows):
                    rim_scr[p, d, i] = found[i * HALO : (i + 1) * HALO, d * LANES : (d + 1) * LANES]
        for k in range(TAPS):
            for d in range(tiles):
                lanes = pl.ds(d * LANES, LANES)
                weight_scr[k, d] = jnp.broadcast_to(weight_ref[k : k + 1, lanes].astype(F32), (8, LANES))
        sum_scr[...] = jnp.zeros_like(sum_scr)
        dcol_scr[...] = jnp.zeros_like(dcol_scr)
        embed_rim(0, 0)

        @pl.loop(0, GROUPS)
        def _(j):
            embed(0, 0, j)
            mixing(0, 0, j)

    def work(slot, more):
        if more:
            embed_rim(row + 1, 1 - slot)
        rim = column_scr[row, pl.ds(HALO - 8, 8)]
        for d in range(tiles):
            conved(slot, HALO - 8, rim, d)

        @pl.loop(0, GROUPS)
        def _(j):
            convolve(slot, j)
            gather(slot, j)
            if more:
                mixing(row + 1, 1 - slot, j)
                embed(row + 1, 1 - slot, j)
            blocks(j)

    last = rows - 1
    pl.when((row < last) & (row % 2 == 0))(lambda: work(0, True))
    pl.when((row < last) & (row % 2 == 1))(lambda: work(1, True))
    pl.when(row == last)(lambda: work(last % 2, False))

    @pl.when(row == rows - 1)
    def _():
        inside = lax.broadcasted_iota(jnp.int32, (rows, padded), 1) < pairs
        turned = jnp.transpose(dcol_scr[...])
        for i in range(rows):
            prod_scr[i, :, pl.ds(0, pairs)] = turned[8 * i : 8 * i + 8]
        products = [prod_scr[:, r] for r in range(REACH)]
        eta = [0.0] * REACH
        for start in range(2):
            inverse = counts(start)
            prob = [prob_scr[start * TAPS + b] for b in range(TAPS)]
            running, grad = 0.0, []
            for b in range(TAPS):
                running = running + keeps(start, b) * products[start + b]
                grad.append(0.5 * running * inverse[b])
            mean = sum(p * g for p, g in zip(prob, grad))
            share = 0.0
            for b in range(TAPS - 1, -1, -1):
                share = share + prob[b] * (grad[b] - mean) * inverse[b]
                eta[start + b] = eta[start + b] + keeps(start, b) * share
        eta = [jnp.where(inside, x, 0.0) for x in eta]
        alpha = [sum(back(eta[r], -(r // 2)) for r in range(parity, REACH, 2)) for parity in range(2)]
        for parity in range(2):
            for k in range(TAPS):
                other = (parity + k) % 2
                ahead = (k + 1 - parity) // 2
                hi = back(alpha[other] * keeps(other, k), -ahead)
                low = hi - hi.astype(BF16).astype(F32)
                hi = hi - low
                for i in range(rows):
                    zeta_scr[i, parity, k : k + 1] = hi[i : i + 1]
                    zeta_scr[i, parity, TAPS + k : TAPS + k + 1] = low[i : i + 1]
        base = lax.broadcasted_iota(jnp.int32, (vocab, padded), 0)

        def scatter(i, total):
            for parity in range(2):
                hot = jnp.where(pick_scr[i, pl.ds(parity, 1)] == base, 1.0, 0.0).astype(BF16)
                total = total + dot_nt(hot, zeta_scr[i, parity].astype(BF16))
            return total

        spread = lax.fori_loop(0, rows, scatter, jnp.zeros((vocab, 2 * TAPS), F32))
        spread = spread[:, :TAPS] + spread[:, TAPS:]
        table = table_ref[...].astype(F32)
        scorer = scorer_ref[...].astype(F32)
        weight = weight_ref[...].astype(F32)
        grad, score_grad, conv = 0.0, 0.0, []
        for k in range(TAPS):
            one = spread[:, k : k + 1]
            total = sum_scr[pl.ds(k * vocab, vocab)] + one * scorer
            grad = grad + weight[k : k + 1] * total
            conv.append(jnp.sum(table * total, axis=0, keepdims=True))
            score_grad = score_grad + weight[k : k + 1] * jnp.sum(table * one, axis=0, keepdims=True)
        table_grad_ref[...] = grad
        rest_ref[...] = jnp.concatenate(conv + [score_grad, jnp.zeros((8 - TAPS - 1, width), F32)], axis=0)


def main(codes, table, conv_weight, scorer, scores, cotangent):
    rows, pairs, width = cotangent.shape
    vocab = table.shape[0]
    assert rows * 8 <= LANES
    padded = -(-pairs // LANES) * LANES + LANES
    tiles = width // LANES
    whole = lambda shape: pl.BlockSpec(shape, lambda i: (0,) * len(shape))
    return pl.pallas_call(
        main_kernel,
        grid=(rows,),
        in_specs=[
            whole(codes.shape),
            whole((vocab, width)),
            whole((TAPS, width)),
            whole((1, width)),
            whole((TAPS, vocab)),
            pl.BlockSpec((1, pairs, width), lambda i: (i, 0, 0)),
        ],
        out_specs=[
            pl.BlockSpec((1, pairs, width), lambda i: (i, 0, 0)),
            whole((vocab, width)),
            whole((8, width)),
        ],
        out_shape=[
            jax.ShapeDtypeStruct((rows, pairs, width), BF16),
            jax.ShapeDtypeStruct((vocab, width), F32),
            jax.ShapeDtypeStruct((8, width), F32),
        ],
        scratch_shapes=[
            pltpu.VMEM((rows, SPAN, padded), jnp.int32),
            pltpu.VMEM((rows, REACH * TAPS, padded), F32),
            pltpu.VMEM((rows, 16, padded), F32),
            pltpu.VMEM((rows, HALO + pairs, 16), F32),
            pltpu.VMEM((2 * TAPS, rows, padded), F32),
            pltpu.VMEM((2 * TAPS, rows, padded), F32),
            pltpu.VMEM((2, tiles, rows, HALO, LANES), F32),
            pltpu.VMEM((2 * tiles * (HALO + pairs), LANES), F32),
            pltpu.VMEM((2 * tiles * (HALO + pairs), LANES), F32),
            pltpu.VMEM((2 * tiles * (HALO + pairs), LANES), F32),
            pltpu.VMEM((pairs, LANES), F32),
            pltpu.VMEM((rows, 8, padded), F32),
            pltpu.VMEM((rows, 2, 2 * TAPS, padded), F32),
            pltpu.VMEM((TAPS, tiles, 8, LANES), F32),
            pltpu.VMEM((TAPS, 2, vocab, pairs), BF16),
            pltpu.VMEM((TAPS, 2, vocab, pairs), BF16),
            pltpu.VMEM((TAPS * vocab, width), F32),
        ],
        name="main",
    )(codes, table, conv_weight, scorer[None], scores, cotangent)


def reduce_all(table_grad, rest, rows_axis, seq_axis):
    ranks, parts = lax.axis_size(rows_axis), lax.axis_size(seq_axis)
    rank, part = lax.axis_index(rows_axis), lax.axis_index(seq_axis)

    def swap(x, axis, stride):
        return lax.ppermute(x, axis, [(i, i ^ stride) for i in range(lax.axis_size(axis))])

    vocab, width = table_grad.shape
    half = width // 2
    core = rank % 2
    whole = jnp.concatenate([table_grad, rest], axis=0)
    mine = lax.dynamic_slice_in_dim(whole, core * half, half, 1)
    other = lax.dynamic_slice_in_dim(whole, (1 - core) * half, half, 1)
    mine = mine + swap(other, rows_axis, 1)
    grad, rest = mine[:vocab], mine[vocab:]
    stride = parts // 2
    while stride:
        size = grad.shape[0] // 2
        bit = (part // stride) % 2
        sent = jnp.concatenate([lax.dynamic_slice_in_dim(grad, (1 - bit) * size, size, 0), rest], axis=0)
        kept = jnp.concatenate([lax.dynamic_slice_in_dim(grad, bit * size, size, 0), rest], axis=0)
        got = kept + swap(sent, seq_axis, stride)
        grad, rest = got[:size], got[size:]
        stride //= 2
    mine = jnp.concatenate([grad, rest], axis=0)
    stride = 2
    while stride < ranks:
        mine = mine + swap(mine, rows_axis, stride)
        stride *= 2
    other = swap(mine, rows_axis, 1)
    both = jnp.where(
        core == 0, jnp.concatenate([mine, other], axis=1), jnp.concatenate([other, mine], axis=1)
    )
    share = vocab // parts
    return both[:share], both[share : share + TAPS], both[share + TAPS]


def per_device(byte_ids, segment_ids, table, conv_weight, scorer, cotangent):
    parts = lax.axis_size("seq")
    codes = jnp.concatenate([byte_ids, segment_ids], axis=0)
    tail = codes[:, -LANES:]
    halo = lax.ppermute(tail, "seq", [(i, i + 1) for i in range(parts - 1)])
    halo = jnp.where(lax.axis_index("seq") == 0, -1, halo)
    scores = score_table(table, conv_weight, scorer)
    codes = jnp.concatenate([halo, codes], axis=1)
    blocks_out, table_grad, rest = main(codes, table, conv_weight, scorer, scores, cotangent)
    table_grad, conv_grad, scorer_grad = reduce_all(table_grad, rest, "rows", "seq")
    return (blocks_out, table_grad, conv_grad, scorer_grad)


def solution(mesh):
    return jax.shard_map(
        per_device,
        mesh=mesh,
        in_specs=(P("rows", "seq"), P("rows", "seq"), P(), P(), P(), P("rows", "seq", None)),
        out_specs=(P("rows", "seq", None), P("seq", None), P(), P()),
        check_vma=False,
    )
```

```python
import functools

import jax
import jax.numpy as jnp
from jax import lax
from jax.experimental import pallas as pl
from jax.experimental.pallas import tpu as pltpu
from jax.sharding import PartitionSpec as P


TAPS = 4
REACH = 5
SPAN = 8
LANES = 128
F32 = jnp.float32
BF16 = jnp.bfloat16
NT = (((1,), (1,)), ((), ()))


def split(x):
    hi = x.astype(BF16)
    return hi, (x - hi.astype(F32)).astype(BF16)


def dot(a, b):
    return jnp.dot(a, b, preferred_element_type=F32)


def dot_nt(a, b):
    return lax.dot_general(a, b, NT, preferred_element_type=F32)


def lanes_of(width):
    step = min(width, LANES)
    return [pl.ds(at, step) for at in range(0, width, step)]


def score_kernel(table_ref, weight_ref, scorer_ref, score_ref):
    hi, lo = split(weight_ref[...].astype(F32) * scorer_ref[...].reshape(1, -1).astype(F32))
    score_ref[...] = dot_nt(hi, table_ref[...]) + dot_nt(lo, table_ref[...])


def score_table(table, conv_weight, scorer):
    return pl.pallas_call(
        score_kernel,
        out_shape=jax.ShapeDtypeStruct((TAPS, table.shape[0]), F32),
        name="score_table",
    )(table, conv_weight, scorer)


def look_up(rows_of, index):
    parts = []
    for at in range(0, index.shape[1], LANES):
        part = index[:, at : at + LANES]
        low = part & (LANES - 1)
        take = lambda h: jnp.take_along_axis(
            jnp.broadcast_to(rows_of[h], part.shape), low, axis=1, mode="promise_in_bounds"
        )
        parts.append(jnp.where(part < LANES, take(0), take(1)))
    return jnp.concatenate(parts, axis=1)


HALO = 16
GROUPS = 1


def main_kernel(
    core_ref, byte_ref, seg_ref, halo_ref, table_ref, weight_ref, scorer_ref, score_ref, cot_ref,
    conv_ref, col_ref, mine_ref, other_ref,
    pick_scr, gam_scr, col_scr, column_scr, keep_scr, prob_scr, rim_scr, emb_a, emb_b, mask_a, mask_b, dcol_scr, prod_scr, zeta_scr,
    weight_scr, mix_a, mix_b, sum_scr,
):
    rows, _, padded = pick_scr.shape
    vocab, width = table_ref.shape
    pairs = cot_ref.shape[1]
    row = pl.program_id(0)
    tiles = width // LANES

    def back(x, n):
        return pltpu.roll(x, n % padded, axis=1) if n % padded else x

    def keeps(parity, k):
        return keep_scr[parity * TAPS + k] if k else 1.0

    def same(r, k):
        return back(keep_scr[r % 2 * TAPS + k], r // 2) if k else 1.0

    def counts(start):
        total, inverse = 1.0, [1.0]
        for b in range(1, TAPS):
            total = total + keeps(start, b)
            inverse.append(1.0 / total)
        return inverse

    def put(scr, q, value):
        for i in range(rows):
            scr[i, pl.ds(q, 1)] = value[i : i + 1]

    @pl.when(row == 0)
    def _():
        halo = halo_ref[...]
        codes = jnp.concatenate(
            [
                jnp.concatenate([halo & (vocab - 1), byte_ref[...]], axis=1),
                jnp.concatenate([halo >> (vocab.bit_length() - 1), seg_ref[...]], axis=1),
            ],
            axis=0,
        )
        codes = codes.astype(F32).astype(BF16)
        reach = codes.shape[1]
        ahead = reach - 2 * pairs
        at = lax.broadcasted_iota(jnp.int32, (reach, padded), 0) - ahead
        lane = lax.broadcasted_iota(jnp.int32, (reach, padded), 1)
        place = at - 2 * jnp.where(lane < pairs, lane, lane - padded)
        byte, seg = [], []
        for parity in range(2):
            found = dot(codes, jnp.where(place == 1 - parity, 1.0, 0.0).astype(BF16))
            byte.append(found[:rows])
            seg.append(found[rows:])
        for parity in range(2):
            put(col_scr, parity, byte[parity])
            for k in range(1, TAPS):
                s = parity + k
                keep = jnp.where(seg[parity] == back(seg[s % 2], s // 2), 1.0, 0.0)
                keep_scr[parity * TAPS + k] = keep
                put(col_scr, 2 + parity * (TAPS - 1) + k - 1, keep)
        byte = [b.astype(jnp.int32) for b in byte]
        for s in range(SPAN):
            put(pick_scr, s, back(byte[s % 2], s // 2))
        found = []
        for k in range(TAPS):
            halves = [score_ref[k : k + 1, h * LANES : (h + 1) * LANES] for h in range(2)]
            found.append([look_up(halves, byte[parity]) for parity in range(2)])
        scored = [
            sum(keeps(parity, k) * back(found[k][(parity + k) % 2], (parity + k) // 2) for k in range(TAPS))
            for parity in range(2)
        ]
        beta = [0.0] * REACH
        for start in range(2):
            inverse = counts(start)
            running, level = 0.0, []
            for b in range(TAPS):
                running = running + keeps(start, b) * back(scored[(start + b) % 2], (start + b) // 2)
                level.append(running * inverse[b])
            top = functools.reduce(jnp.maximum, level)
            level = [jnp.exp(x - top) for x in level]
            norm = 1.0 / sum(level)
            level = [x * norm for x in level]
            share = 0.0
            for b in range(TAPS - 1, -1, -1):
                prob_scr[start * TAPS + b] = level[b]
                share = share + level[b] * inverse[b]
                beta[start + b] = beta[start + b] + 0.5 * keeps(start, b) * share
        for r in range(REACH):
            put(col_scr, 2 * TAPS + r, beta[r])
            for k in range(TAPS):
                put(gam_scr, r * TAPS + k, beta[r] * same(r, k))

    deep = HALO + pairs
    group = pairs // GROUPS
    part_v = vocab // GROUPS

    embs, masks, mixes = (emb_a, emb_b), (mask_a, mask_b), (mix_a, mix_b)

    def spot(parity, d):
        return (parity * tiles + d) * deep

    def embed(i, slot, j):
        at = pl.multiple_of(HALO + j * group, 8)
        column = column_scr[i, pl.ds(at, group)]
        value = lax.broadcasted_iota(jnp.int32, (group, vocab), 1).astype(F32)
        hot = [jnp.where(column[:, p : p + 1] == value, 1.0, 0.0).astype(BF16) for p in range(2)]
        found = dot(jnp.concatenate(hot, axis=0), table_ref[...])
        for p in range(2):
            for d in range(tiles):
                to = pl.multiple_of(spot(p, d) + at, 8)
                embs[slot][pl.ds(to, group)] = found[p * group : (p + 1) * group, d * LANES : (d + 1) * LANES]

    def embed_rim(i, slot):
        for p in range(2):
            for d in range(tiles):
                to = pl.multiple_of(spot(p, d), 8)
                embs[slot][pl.ds(to, HALO)] = rim_scr[p, d, i]

    def mixing(i, slot, j):
        for lane in lanes_of(pairs):
            size = lane.size
            byte = [pick_scr[i, pl.ds(s, 1), lane] for s in range(SPAN)]
            gam = [gam_scr[i, pl.ds(q, 1), lane] for q in range(REACH * TAPS)]
            base = lax.broadcasted_iota(jnp.int32, (16, size), 0) + j * part_v
            for v in range(0, part_v, 16):
                hit = [b == base + v for b in byte]
                at = pl.ds(pl.multiple_of(j * part_v + v, 16), 16)
                for k in range(TAPS):
                    mixed = sum(jnp.where(hit[r + k], gam[r * TAPS + k], 0.0) for r in range(REACH))
                    hi, lo = split(mixed)
                    mixes[slot][k, 0, at, lane] = hi
                    mixes[slot][k, 1, at, lane] = lo

    def gather(slot, j, first):
        cot = cot_ref[0]
        at = pl.ds(pl.multiple_of(j * part_v, 16), part_v)
        hi = jnp.concatenate([mixes[slot][k, 0, at] for k in range(TAPS)], axis=0)
        lo = jnp.concatenate([mixes[slot][k, 1, at] for k in range(TAPS)], axis=0)
        if pairs % LANES == 0:
            part = dot(jnp.concatenate([hi, lo], axis=1), jnp.concatenate([cot, cot], axis=0))
        else:
            part = dot(hi, cot) + dot(lo, cot)
        for k in range(TAPS):
            to = pl.ds(pl.multiple_of(k * vocab + j * part_v, 8), part_v)
            more = part[k * part_v : (k + 1) * part_v]
            sum_scr[to] = more if first else sum_scr[to] + more

    def spread(i, slot, at, to, size):
        for t in range(0, size, 8):
            column = column_scr[i, pl.ds(pl.multiple_of(at + t, 8), 8)]
            for q in range(2 * (TAPS - 1)):
                place = pl.multiple_of(q * (8 + pairs) + to + t, 8)
                masks[slot][pl.ds(place, 8)] = jnp.broadcast_to(column[:, 2 + q : 3 + q], (8, LANES))

    def conved(slot, at):
        keep = [
            masks[slot][pl.ds(pl.multiple_of(q * (8 + pairs) + at - HALO + 8, 8), 8)] for q in range(2 * (TAPS - 1))
        ]
        for d in range(tiles):
            taken = [embs[slot][pl.ds(spot(s % 2, d) + at - s // 2, 8)] for s in range(REACH)]
            for p in range(2):
                total = weight_scr[0, d] * taken[p]
                for k in range(1, TAPS):
                    total = total + keep[p * (TAPS - 1) + k - 1] * (weight_scr[k, d] * taken[p + k])
                conv_ref[pl.ds(pl.multiple_of(spot(p, d) + at, 8), 8)] = total

    lane_at = lax.broadcasted_iota(jnp.int32, (8, LANES), 1) - 8 * row

    def convolve(slot, j):
        for t in range(0, group, 8):
            conved(slot, pl.multiple_of(HALO + j * group + t, 8))

    def products(j):
        for t in range(0, group, 16):
            start = pl.multiple_of(j * group + t, 16)
            total = [[0.0] * REACH for _ in range(2)]
            for d in range(tiles):
                grad = cot_ref[0, pl.ds(start, 16), pl.ds(d * LANES, LANES)].astype(F32)
                for u in range(2):
                    at = HALO + start + 8 * u
                    for r in range(REACH):
                        conv = conv_ref[pl.ds(spot(r % 2, d) + at - r // 2, 8)]
                        total[u][r] = total[u][r] + grad[8 * u : 8 * u + 8] * conv
            for u in range(2):
                to = pl.ds(pl.multiple_of(start + 8 * u, 8), 8)
                found = dcol_scr[to]
                for r in range(REACH):
                    found = jnp.where(lane_at == r, jnp.sum(total[u][r], axis=1, keepdims=True), found)
                dcol_scr[to] = found

    @pl.when(row == 0)
    def _():
        for i in range(rows):
            column = jnp.transpose(col_scr[i])
            column_scr[i, pl.ds(0, HALO)] = column[padded - HALO :]
            column_scr[i, pl.ds(HALO, pairs)] = column[:pairs]
        value = lax.broadcasted_iota(jnp.int32, (HALO, vocab), 1).astype(F32)
        for p in range(2):
            hot = [
                jnp.where(column_scr[i, pl.ds(0, HALO)][:, p : p + 1] == value, 1.0, 0.0).astype(BF16)
                for i in range(rows)
            ]
            found = dot(jnp.concatenate(hot, axis=0), table_ref[...])
            for d in range(tiles):
                for i in range(rows):
                    rim_scr[p, d, i] = found[i * HALO : (i + 1) * HALO, d * LANES : (d + 1) * LANES]
        for k in range(TAPS):
            for d in range(tiles):
                lanes = pl.ds(d * LANES, LANES)
                weight_scr[k, d] = jnp.broadcast_to(weight_ref[k : k + 1, lanes].astype(F32), (8, LANES))
        dcol_scr[...] = jnp.zeros_like(dcol_scr)
        embed_rim(0, 0)
        spread(0, 0, HALO - 8, 0, 8)
        col_ref[...] = col_scr[...]

        @pl.loop(0, GROUPS)
        def _(j):
            spread(0, 0, HALO + j * group, 8 + j * group, group)
            embed(0, 0, j)
            mixing(0, 0, j)

    def work(slot, more, first=False):
        if more:
            embed_rim(row + 1, 1 - slot)
            spread(row + 1, 1 - slot, HALO - 8, 0, 8)
        conved(slot, HALO - 8)

        @pl.loop(0, GROUPS)
        def _(j):
            convolve(slot, j)
            gather(slot, j, first)
            if more:
                spread(row + 1, 1 - slot, HALO + j * group, 8 + j * group, group)
                mixing(row + 1, 1 - slot, j)
                embed(row + 1, 1 - slot, j)
            products(j)

    last = rows - 1
    pl.when(row == 0)(lambda: work(0, last > 0, True))
    pl.when((row > 0) & (row < last) & (row % 2 == 0))(lambda: work(0, True))
    pl.when((row < last) & (row % 2 == 1))(lambda: work(1, True))
    pl.when((row > 0) & (row == last))(lambda: work(last % 2, False))

    @pl.when(row == rows - 1)
    def _():
        inside = lax.broadcasted_iota(jnp.int32, (rows, padded), 1) < pairs
        turned = jnp.transpose(dcol_scr[...])
        for i in range(rows):
            prod_scr[i, :, pl.ds(0, pairs)] = turned[8 * i : 8 * i + 8]
        products = [prod_scr[:, r] for r in range(REACH)]
        eta = [0.0] * REACH
        for start in range(2):
            inverse = counts(start)
            prob = [prob_scr[start * TAPS + b] for b in range(TAPS)]
            running, grad = 0.0, []
            for b in range(TAPS):
                running = running + keeps(start, b) * products[start + b]
                grad.append(0.5 * running * inverse[b])
            mean = sum(p * g for p, g in zip(prob, grad))
            share = 0.0
            for b in range(TAPS - 1, -1, -1):
                share = share + prob[b] * (grad[b] - mean) * inverse[b]
                eta[start + b] = eta[start + b] + keeps(start, b) * share
        eta = [jnp.where(inside, x, 0.0) for x in eta]
        alpha = [sum(back(eta[r], -(r // 2)) for r in range(parity, REACH, 2)) for parity in range(2)]
        for parity in range(2):
            for k in range(TAPS):
                other = (parity + k) % 2
                ahead = (k + 1 - parity) // 2
                hi = back(alpha[other] * keeps(other, k), -ahead)
                low = hi - hi.astype(BF16).astype(F32)
                hi = hi - low
                for i in range(rows):
                    zeta_scr[i, parity, k : k + 1] = hi[i : i + 1]
                    zeta_scr[i, parity, TAPS + k : TAPS + k + 1] = low[i : i + 1]
        base = lax.broadcasted_iota(jnp.int32, (vocab, padded), 0)

        found = jnp.zeros((vocab, 2 * TAPS), F32)
        for i in range(rows):
            hot = [jnp.where(pick_scr[i, pl.ds(p, 1)] == base, 1.0, 0.0).astype(BF16) for p in range(2)]
            found = found + dot_nt(
                jnp.concatenate(hot, axis=1),
                jnp.concatenate([zeta_scr[i, p].astype(BF16) for p in range(2)], axis=1),
            )
        found = found[:, :TAPS] + found[:, TAPS:]
        scorer = scorer_ref[...].reshape(1, -1).astype(F32)
        weight = weight_ref[...].astype(F32)
        table = table_ref[...].astype(F32)
        hi, lo = split(found)
        tall = lambda a, b: lax.dot_general(a, b, (((0,), (0,)), ((), ())), preferred_element_type=F32)
        sums = tall(hi, table_ref[...]) + tall(lo, table_ref[...])
        near, rest = split(weight * scorer)
        grad = dot(
            jnp.concatenate([hi, lo, hi], axis=1), jnp.concatenate([near, near, rest], axis=0)
        )
        conv, score_grad = [], 0.0
        for k in range(TAPS):
            total = sum_scr[pl.ds(k * vocab, vocab)]
            grad = grad + weight[k : k + 1] * total
            conv.append(jnp.sum(table * total, axis=0, keepdims=True) + scorer * sums[k : k + 1])
            score_grad = score_grad + weight[k : k + 1] * sums[k : k + 1]
        rest = jnp.concatenate(conv + [score_grad, jnp.zeros((8 - TAPS - 1, width), F32)], axis=0)
        half = width // 2
        first = core_ref[0] == 0
        for at, value in ((0, grad), (vocab, rest)):
            to = pl.ds(at, value.shape[0])
            left, right = value[:, :half], value[:, half:]
            mine_ref[to] = jnp.where(first, left, right)
            other_ref[to] = jnp.where(first, right, left)


def blocks_kernel(*refs):
    conv_refs, col_ref, out_ref = refs[: 2 * STREAMS], refs[2 * STREAMS], refs[-1]
    pairs, width = out_ref.shape[1:]
    column = jnp.transpose(col_ref[0])
    each = width // LANES // STREAMS
    for t in range(0, pairs, 16):
        share = [
            [jnp.broadcast_to(column[t + u : t + u + 8, q : q + 1], (8, LANES)) for q in range(2 * TAPS, 2 * TAPS + REACH)]
            for u in (0, 8)
        ]
        for d in range(width // LANES):
            out = []
            for u in range(2):
                total = 0.0
                for r in range(REACH):
                    at = d % each * (HALO + pairs) + HALO + t + 8 * u - r // 2
                    total = total + share[u][r] * conv_refs[r % 2 * STREAMS + d // each][0, 0, pl.ds(at, 8)]
                out.append(total)
            out_ref[0, pl.ds(t, 16), pl.ds(d * LANES, LANES)] = jnp.concatenate(out, axis=0).astype(BF16)


STREAMS = 3


def blocks(conv, columns, pairs, width, start, stop, before=None):
    rows = conv.shape[0]
    conv = conv.reshape(rows, 2 * STREAMS, -1, LANES)
    part = lambda n: pl.BlockSpec((1, 1) + conv.shape[2:], lambda i: (i + start, n, 0, 0))
    return pl.pallas_call(
        blocks_kernel,
        grid=(stop - start,),
        in_specs=[part(n) for n in range(2 * STREAMS)]
        + [pl.BlockSpec((1,) + columns.shape[1:], lambda i: (i + start, 0, 0))]
        + ([] if before is None else [pl.BlockSpec(memory_space=pl.ANY)]),
        out_specs=pl.BlockSpec((1, pairs, width), lambda i: (i + start, 0, 0)),
        out_shape=jax.ShapeDtypeStruct((rows, pairs, width), BF16),
        input_output_aliases={} if before is None else {2 * STREAMS + 1: 0},
        cost_estimate=pl.CostEstimate(
            flops=9 * (stop - start) * pairs * width,
            bytes_accessed=(stop - start) * (4 * conv.size // rows + 2 * pairs * width),
            transcendentals=0,
        ),
        name="blocks",
    )(*[conv] * (2 * STREAMS), columns, *([] if before is None else [before]))


def main(core, byte_ids, segment_ids, halo, table, conv_weight, scorer, scores, cotangent):
    rows, pairs, width = cotangent.shape
    vocab = table.shape[0]
    assert rows * 8 <= LANES
    padded = -(-pairs // LANES) * LANES + LANES
    tiles = width // LANES
    whole = lambda shape: pl.BlockSpec(shape, lambda i: (0,) * len(shape))
    return pl.pallas_call(
        main_kernel,
        grid=(rows,),
        in_specs=[
            pl.BlockSpec(memory_space=pltpu.SMEM),
            whole(byte_ids.shape),
            whole(segment_ids.shape),
            whole(halo.shape),
            whole((vocab, width)),
            whole((TAPS, width)),
            whole((width,)),
            whole((TAPS, vocab)),
            pl.BlockSpec((1, pairs, width), lambda i: (i, 0, 0)),
        ],
        out_specs=[
            pl.BlockSpec((None, 2 * tiles * (HALO + pairs), LANES), lambda i: (i, 0, 0)),
            whole((rows, 16, padded)),
            whole((vocab + 8, width // 2)),
            whole((vocab + 8, width // 2)),
        ],
        out_shape=[
            jax.ShapeDtypeStruct((rows, 2 * tiles * (HALO + pairs), LANES), F32),
            jax.ShapeDtypeStruct((rows, 16, padded), F32),
            jax.ShapeDtypeStruct((vocab + 8, width // 2), F32),
            jax.ShapeDtypeStruct((vocab + 8, width // 2), F32),
        ],
        scratch_shapes=[
            pltpu.VMEM((rows, SPAN, padded), jnp.int32),
            pltpu.VMEM((rows, REACH * TAPS, padded), F32),
            pltpu.VMEM((rows, 16, padded), F32),
            pltpu.VMEM((rows, HALO + pairs, 16), F32),
            pltpu.VMEM((2 * TAPS, rows, padded), F32),
            pltpu.VMEM((2 * TAPS, rows, padded), F32),
            pltpu.VMEM((2, tiles, rows, HALO, LANES), F32),
            pltpu.VMEM((2 * tiles * (HALO + pairs), LANES), F32),
            pltpu.VMEM((2 * tiles * (HALO + pairs), LANES), F32),
            pltpu.VMEM((2 * (TAPS - 1) * (8 + pairs), LANES), F32),
            pltpu.VMEM((2 * (TAPS - 1) * (8 + pairs), LANES), F32),
            pltpu.VMEM((pairs, LANES), F32),
            pltpu.VMEM((rows, 8, padded), F32),
            pltpu.VMEM((rows, 2, 2 * TAPS, padded), F32),
            pltpu.VMEM((TAPS, tiles, 8, LANES), F32),
            pltpu.VMEM((TAPS, 2, vocab, pairs), BF16),
            pltpu.VMEM((TAPS, 2, vocab, pairs), BF16),
            pltpu.VMEM((TAPS * vocab, width), F32),
        ],
        name="main",
    )(core, byte_ids, segment_ids, halo, table, conv_weight, scorer, scores, cotangent)


def add_parts(mine, other, rows_axis, seq_axis, vocab):
    ranks, parts = lax.axis_size(rows_axis), lax.axis_size(seq_axis)
    rank, part = lax.axis_index(rows_axis), lax.axis_index(seq_axis)
    share = vocab // parts

    def swap(x, stride):
        return lax.ppermute(x, rows_axis, [(i, i ^ stride) for i in range(ranks)])

    mine = mine + swap(other, 1)
    rest = mine[vocab:]
    piece = lambda n: jnp.concatenate(
        [lax.dynamic_slice_in_dim(mine, (part + n) % parts * share, share, 0), rest], axis=0
    )
    total = piece(0)
    for n in range(1, parts):
        total = total + lax.ppermute(piece(n), seq_axis, [(i, (i + n) % parts) for i in range(parts)])
    stride = 2
    while stride < ranks:
        total = total + swap(total, stride)
        stride *= 2
    other = swap(total, 1)
    whole = jnp.where(
        rank % 2 == 0, jnp.concatenate([total, other], axis=1), jnp.concatenate([other, total], axis=1)
    )
    return whole[:share], whole[share : share + TAPS], whole[share + TAPS]


def per_device(byte_ids, segment_ids, table, conv_weight, scorer, cotangent):
    parts = lax.axis_size("seq")
    vocab = table.shape[0]
    rows, pairs, width = cotangent.shape
    tail = byte_ids[:, -LANES:] + vocab * segment_ids[:, -LANES:]
    halo = lax.ppermute(tail, "seq", [(i, i + 1) for i in range(parts - 1)])
    halo = jnp.where(lax.axis_index("seq") == 0, -vocab, halo)
    core = (lax.axis_index("rows") % 2)[None]
    scores = score_table(table, conv_weight, scorer)
    conv, columns, mine, other = main(core, byte_ids, segment_ids, halo, table, conv_weight, scorer, scores, cotangent)
    cuts = (0, rows // 2, rows - rows // 4, rows)
    out = None
    for n in range(3):
        out = blocks(conv, columns, pairs, width, cuts[n], cuts[n + 1], out)
    table_grad, conv_grad, scorer_grad = add_parts(mine, other, "rows", "seq", vocab)
    return (out, table_grad, conv_grad, scorer_grad)


def solution(mesh):
    return jax.shard_map(
        per_device,
        mesh=mesh,
        in_specs=(P("rows", "seq"), P("rows", "seq"), P(), P(), P(), P("rows", "seq", None)),
        out_specs=(P("rows", "seq", None), P("seq", None), P(), P()),
        check_vma=False,
    )
```

```python
import functools

import jax
import jax.numpy as jnp
from jax import lax
from jax.experimental import pallas as pl
from jax.experimental.pallas import tpu as pltpu
from jax.sharding import PartitionSpec as P


TAPS = 4
REACH = 5
SPAN = 8
LANES = 128
F32 = jnp.float32
BF16 = jnp.bfloat16
NT = (((1,), (1,)), ((), ()))


def split(x):
    hi = x.astype(BF16)
    return hi, (x - hi.astype(F32)).astype(BF16)


def dot(a, b):
    return jnp.dot(a, b, preferred_element_type=F32)


def dot_nt(a, b):
    return lax.dot_general(a, b, NT, preferred_element_type=F32)


def lanes_of(width):
    step = min(width, LANES)
    return [pl.ds(at, step) for at in range(0, width, step)]


def score_kernel(table_ref, weight_ref, scorer_ref, score_ref):
    hi, lo = split(weight_ref[...].astype(F32) * scorer_ref[...].reshape(1, -1).astype(F32))
    score_ref[...] = dot_nt(hi, table_ref[...]) + dot_nt(lo, table_ref[...])


def score_table(table, conv_weight, scorer):
    return pl.pallas_call(
        score_kernel,
        out_specs=pl.BlockSpec(memory_space=pltpu.VMEM),
        out_shape=jax.ShapeDtypeStruct((TAPS, table.shape[0]), F32),
        name="score_table",
    )(table, conv_weight, scorer)


def look_up(rows_of, index):
    parts = []
    for at in range(0, index.shape[1], LANES):
        part = index[:, at : at + LANES]
        low = part & (LANES - 1)
        take = lambda h: jnp.take_along_axis(
            jnp.broadcast_to(rows_of[h], part.shape), low, axis=1, mode="promise_in_bounds"
        )
        parts.append(jnp.where(part < LANES, take(0), take(1)))
    return jnp.concatenate(parts, axis=1)


HALO = 16
GROUPS = 1


def main_kernel(
    byte_ref, seg_ref, halo_ref, table_ref, weight_ref, scorer_ref, score_ref, cot_ref,
    conv_ref, col_ref, mine_ref, other_ref,
    line_scr, hot_scr, col_scr, column_scr, keep_scr, prob_scr, rim_scr, emb_a, emb_b, mask_a, mask_b, dcol_scr, prod_scr, zeta_scr,
    weight_scr, mix_a, mix_b, sum_scr,
):
    rows, _, padded = col_scr.shape
    vocab, width = table_ref.shape
    pairs = cot_ref.shape[1]
    row = pl.program_id(0)
    tiles = width // LANES

    def back(x, n):
        return pltpu.roll(x, n % padded, axis=1) if n % padded else x

    def keeps(parity, k):
        return keep_scr[parity * TAPS + k] if k else 1.0

    def same(r, k):
        return back(keep_scr[r % 2 * TAPS + k], r // 2) if k else 1.0

    def counts(start):
        total, inverse = 1.0, [1.0]
        for b in range(1, TAPS):
            total = total + keeps(start, b)
            inverse.append(1.0 / total)
        return inverse

    def put(scr, q, value):
        for i in range(rows):
            scr[i, pl.ds(q, 1)] = value[i : i + 1]

    def line(q, tile, i):
        return (q * (padded // LANES) + tile) * rows + i

    def lay(q, value):
        for tile in range(padded // LANES):
            line_scr[pl.ds(line(q, tile, 0), rows)] = value[:, tile * LANES : (tile + 1) * LANES]

    @pl.when(row == 0)
    def _():
        halo = jnp.where(lax.axis_index("seq") == 0, -vocab, halo_ref[...])
        codes = jnp.concatenate(
            [
                jnp.concatenate([halo & (vocab - 1), byte_ref[...]], axis=1),
                jnp.concatenate([halo >> (vocab.bit_length() - 1), seg_ref[...]], axis=1),
            ],
            axis=0,
        )
        codes = codes.astype(F32).astype(BF16)
        reach = codes.shape[1]
        ahead = reach - 2 * pairs
        at = lax.broadcasted_iota(jnp.int32, (reach, padded), 0) - ahead
        lane = lax.broadcasted_iota(jnp.int32, (reach, padded), 1)
        place = at - 2 * jnp.where(lane < pairs, lane, lane - padded)
        byte, seg = [], []
        for parity in range(2):
            found = dot(codes, jnp.where(place == 1 - parity, 1.0, 0.0).astype(BF16))
            byte.append(found[:rows])
            seg.append(found[rows:])
        for parity in range(2):
            put(col_scr, parity, byte[parity])
            for k in range(1, TAPS):
                s = parity + k
                keep = jnp.where(seg[parity] == back(seg[s % 2], s // 2), 1.0, 0.0)
                keep_scr[parity * TAPS + k] = keep
                put(col_scr, 2 + parity * (TAPS - 1) + k - 1, keep)
        bytes_at = [back(byte[s % 2], s // 2) for s in range(SPAN)]
        byte = [b.astype(jnp.int32) for b in byte]
        for s in range(SPAN):
            lay(s, bytes_at[s])
        found = []
        for k in range(TAPS):
            halves = [score_ref[k : k + 1, h * LANES : (h + 1) * LANES] for h in range(2)]
            found.append([look_up(halves, byte[parity]) for parity in range(2)])
        scored = [
            sum(keeps(parity, k) * back(found[k][(parity + k) % 2], (parity + k) // 2) for k in range(TAPS))
            for parity in range(2)
        ]
        beta = [0.0] * REACH
        for start in range(2):
            inverse = counts(start)
            running, level = 0.0, []
            for b in range(TAPS):
                running = running + keeps(start, b) * back(scored[(start + b) % 2], (start + b) // 2)
                level.append(running * inverse[b])
            top = functools.reduce(jnp.maximum, level)
            level = [jnp.exp(x - top) for x in level]
            norm = 1.0 / sum(level)
            level = [x * norm for x in level]
            share = 0.0
            for b in range(TAPS - 1, -1, -1):
                prob_scr[start * TAPS + b] = level[b]
                share = share + level[b] * inverse[b]
                beta[start + b] = beta[start + b] + 0.5 * keeps(start, b) * share
        alike = {
            (s, u): bytes_at[s] == bytes_at[u] for s in range(SPAN) for u in range(s + 1, min(s + REACH, SPAN))
        }
        for r in range(REACH):
            put(col_scr, 2 * TAPS + r, beta[r])
        for k in range(TAPS):
            alone = [beta[r] * same(r, k) for r in range(REACH)]
            for r in range(REACH):
                total = alone[r]
                for u in range(REACH):
                    if u != r:
                        total = total + jnp.where(alike[min(r, u) + k, max(r, u) + k], alone[u], 0.0)
                hi = total.astype(BF16).astype(F32)
                lay(SPAN + 2 * (r * TAPS + k), hi)
                lay(SPAN + 2 * (r * TAPS + k) + 1, total - hi)

    deep = HALO + pairs
    group = pairs // GROUPS
    part_v = vocab // GROUPS

    embs, masks, mixes = (emb_a, emb_b), (mask_a, mask_b), (mix_a, mix_b)

    def spot(parity, d):
        return (parity * tiles + d) * deep

    def embed(i, slot, j):
        at = pl.multiple_of(HALO + j * group, 8)
        column = column_scr[i, pl.ds(at, group)]
        value = lax.broadcasted_iota(jnp.int32, (group, vocab), 1).astype(F32)
        hot = [jnp.where(column[:, p : p + 1] == value, 1.0, 0.0).astype(BF16) for p in range(2)]
        for p in range(2):
            hot_scr[i, p, pl.ds(j * group, group)] = hot[p]
        found = dot(jnp.concatenate(hot, axis=0), table_ref[...])
        for p in range(2):
            for d in range(tiles):
                to = pl.multiple_of(spot(p, d) + at, 8)
                embs[slot][pl.ds(to, group)] = found[p * group : (p + 1) * group, d * LANES : (d + 1) * LANES]

    def embed_rim(i, slot):
        for p in range(2):
            for d in range(tiles):
                to = pl.multiple_of(spot(p, d), 8)
                embs[slot][pl.ds(to, HALO)] = rim_scr[p, d, i]

    def mixing(i, slot, j):
        deep_v = 32
        for tile, lane in enumerate(lanes_of(pairs)):
            size = lane.size

            def full(q):
                return jnp.broadcast_to(line_scr[pl.ds(line(q, tile, i), 1)][:, :size], (deep_v, size)).astype(BF16)

            byte = [full(s) for s in range(SPAN)]
            base = lax.broadcasted_iota(jnp.int32, (deep_v, size), 0).astype(F32).astype(BF16)
            for v in range(0, part_v, deep_v):
                value = base + (j * part_v + v)
                hit = [b == value for b in byte]
                at = pl.ds(j * part_v + v, deep_v)
                for k in range(TAPS):
                    for half in range(2):
                        mixed = jnp.zeros((deep_v, size), BF16)
                        for r in range(REACH):
                            mixed = jnp.where(hit[r + k], full(SPAN + 2 * (r * TAPS + k) + half), mixed)
                        mixes[slot][k, half, at, lane] = mixed

    def gather(slot, j, first):
        cot = cot_ref[0]
        at = pl.ds(pl.multiple_of(j * part_v, 16), part_v)
        hi = jnp.concatenate([mixes[slot][k, 0, at] for k in range(TAPS)], axis=0)
        lo = jnp.concatenate([mixes[slot][k, 1, at] for k in range(TAPS)], axis=0)
        if pairs % LANES == 0:
            part = dot(jnp.concatenate([hi, lo], axis=1), jnp.concatenate([cot, cot], axis=0))
        else:
            part = dot(hi, cot) + dot(lo, cot)
        for k in range(TAPS):
            to = pl.ds(pl.multiple_of(k * vocab + j * part_v, 8), part_v)
            more = part[k * part_v : (k + 1) * part_v]
            sum_scr[to] = more if first else sum_scr[to] + more

    def spread(i, slot, at, to, size):
        for t in range(0, size, 8):
            column = column_scr[i, pl.ds(pl.multiple_of(at + t, 8), 8)]
            for q in range(2 * (TAPS - 1)):
                place = pl.multiple_of(q * (8 + pairs) + to + t, 8)
                masks[slot][pl.ds(place, 8)] = jnp.broadcast_to(column[:, 2 + q : 3 + q], (8, LANES))

    def conved(slot, at):
        keep = [
            masks[slot][pl.ds(pl.multiple_of(q * (8 + pairs) + at - HALO + 8, 8), 8)] for q in range(2 * (TAPS - 1))
        ]
        for d in range(tiles):
            taken = [embs[slot][pl.ds(spot(s % 2, d) + at - s // 2, 8)] for s in range(REACH)]
            for p in range(2):
                total = weight_scr[0, d] * taken[p]
                for k in range(1, TAPS):
                    total = total + keep[p * (TAPS - 1) + k - 1] * (weight_scr[k, d] * taken[p + k])
                conv_ref[pl.ds(pl.multiple_of(spot(p, d) + at, 8), 8)] = total

    lane_at = lax.broadcasted_iota(jnp.int32, (8, LANES), 1) - 8 * row

    def convolve(slot, j):
        for t in range(0, group, 8):
            conved(slot, pl.multiple_of(HALO + j * group + t, 8))

    def products(j):
        for t in range(0, group, 16):
            start = pl.multiple_of(j * group + t, 16)
            total = [[0.0] * REACH for _ in range(2)]
            for d in range(tiles):
                grad = cot_ref[0, pl.ds(start, 16), pl.ds(d * LANES, LANES)].astype(F32)
                for u in range(2):
                    at = HALO + start + 8 * u
                    for r in range(REACH):
                        conv = conv_ref[pl.ds(spot(r % 2, d) + at - r // 2, 8)]
                        total[u][r] = total[u][r] + grad[8 * u : 8 * u + 8] * conv
            for u in range(2):
                to = pl.ds(pl.multiple_of(start + 8 * u, 8), 8)
                found = dcol_scr[to]
                for r in range(REACH):
                    found = jnp.where(lane_at == r, jnp.sum(total[u][r], axis=1, keepdims=True), found)
                dcol_scr[to] = found

    @pl.when(row == 0)
    def _():
        for i in range(rows):
            column = jnp.transpose(col_scr[i])
            column_scr[i, pl.ds(0, HALO)] = column[padded - HALO :]
            column_scr[i, pl.ds(HALO, pairs)] = column[:pairs]
        value = lax.broadcasted_iota(jnp.int32, (HALO, vocab), 1).astype(F32)
        for p in range(2):
            hot = [
                jnp.where(column_scr[i, pl.ds(0, HALO)][:, p : p + 1] == value, 1.0, 0.0).astype(BF16)
                for i in range(rows)
            ]
            for i in range(rows):
                hot_scr[i, p, pl.ds(pairs, padded - HALO - pairs)] = jnp.zeros((padded - HALO - pairs, vocab), BF16)
                hot_scr[i, p, pl.ds(padded - HALO, HALO)] = hot[i]
            found = dot(jnp.concatenate(hot, axis=0), table_ref[...])
            for d in range(tiles):
                for i in range(rows):
                    rim_scr[p, d, i] = found[i * HALO : (i + 1) * HALO, d * LANES : (d + 1) * LANES]
        for k in range(TAPS):
            for d in range(tiles):
                lanes = pl.ds(d * LANES, LANES)
                weight_scr[k, d] = jnp.broadcast_to(weight_ref[k : k + 1, lanes].astype(F32), (8, LANES))
        dcol_scr[...] = jnp.zeros_like(dcol_scr)
        embed_rim(0, 0)
        spread(0, 0, HALO - 8, 0, 8)
        col_ref[...] = col_scr[...]

        @pl.loop(0, GROUPS)
        def _(j):
            spread(0, 0, HALO + j * group, 8 + j * group, group)
            embed(0, 0, j)
            mixing(0, 0, j)

    def work(slot, more, first=False):
        if more:
            embed_rim(row + 1, 1 - slot)
            spread(row + 1, 1 - slot, HALO - 8, 0, 8)
        conved(slot, HALO - 8)

        @pl.loop(0, GROUPS)
        def _(j):
            convolve(slot, j)
            gather(slot, j, first)
            if more:
                spread(row + 1, 1 - slot, HALO + j * group, 8 + j * group, group)
                mixing(row + 1, 1 - slot, j)
                embed(row + 1, 1 - slot, j)
            products(j)

    last = rows - 1
    pl.when(row == 0)(lambda: work(0, last > 0, True))
    pl.when((row > 0) & (row < last) & (row % 2 == 0))(lambda: work(0, True))
    pl.when((row < last) & (row % 2 == 1))(lambda: work(1, True))
    pl.when((row > 0) & (row == last))(lambda: work(last % 2, False))

    @pl.when(row == rows - 1)
    def _():
        inside = lax.broadcasted_iota(jnp.int32, (rows, padded), 1) < pairs
        turned = jnp.transpose(dcol_scr[...])
        for i in range(rows):
            prod_scr[i, :, pl.ds(0, pairs)] = turned[8 * i : 8 * i + 8]
        products = [prod_scr[:, r] for r in range(REACH)]
        eta = [0.0] * REACH
        for start in range(2):
            inverse = counts(start)
            prob = [prob_scr[start * TAPS + b] for b in range(TAPS)]
            running, grad = 0.0, []
            for b in range(TAPS):
                running = running + keeps(start, b) * products[start + b]
                grad.append(0.5 * running * inverse[b])
            mean = sum(p * g for p, g in zip(prob, grad))
            share = 0.0
            for b in range(TAPS - 1, -1, -1):
                share = share + prob[b] * (grad[b] - mean) * inverse[b]
                eta[start + b] = eta[start + b] + keeps(start, b) * share
        eta = [jnp.where(inside, x, 0.0) for x in eta]
        alpha = [sum(back(eta[r], -(r // 2)) for r in range(parity, REACH, 2)) for parity in range(2)]
        for parity in range(2):
            for k in range(TAPS):
                other = (parity + k) % 2
                ahead = (k + 1 - parity) // 2
                hi = back(alpha[other] * keeps(other, k), -ahead)
                low = hi - hi.astype(BF16).astype(F32)
                hi = hi - low
                for i in range(rows):
                    zeta_scr[i, parity, k : k + 1] = hi[i : i + 1]
                    zeta_scr[i, parity, TAPS + k : TAPS + k + 1] = low[i : i + 1]
        found = jnp.zeros((2 * TAPS, vocab), F32)
        for i in range(rows):
            for p in range(2):
                found = found + dot(zeta_scr[i, p].astype(BF16), hot_scr[i, p])
        found = found[:TAPS] + found[TAPS:]
        scorer = scorer_ref[...].reshape(1, -1).astype(F32)
        weight = weight_ref[...].astype(F32)
        table = table_ref[...].astype(F32)
        hi, lo = split(found)
        sums = dot(hi, table_ref[...]) + dot(lo, table_ref[...])
        hi, lo = hi.astype(F32), lo.astype(F32)
        near, rest = split(weight * scorer)
        near, rest = near.astype(F32), rest.astype(F32)
        grad = lax.dot_general(
            jnp.concatenate([hi, lo, hi], axis=0).astype(BF16),
            jnp.concatenate([near, near, rest], axis=0).astype(BF16),
            (((0,), (0,)), ((), ())),
            preferred_element_type=F32,
        )
        conv, score_grad = [], 0.0
        for k in range(TAPS):
            total = sum_scr[pl.ds(k * vocab, vocab)]
            grad = grad + weight[k : k + 1] * total
            conv.append(jnp.sum(table * total, axis=0, keepdims=True) + scorer * sums[k : k + 1])
            score_grad = score_grad + weight[k : k + 1] * sums[k : k + 1]
        rest = jnp.concatenate(conv + [score_grad, jnp.zeros((8 - TAPS - 1, width), F32)], axis=0)
        half = width // 2
        first = lax.axis_index("rows") % 2 == 0
        for at, value in ((0, grad), (vocab, rest)):
            to = pl.ds(at, value.shape[0])
            left, right = value[:, :half], value[:, half:]
            mine_ref[to] = jnp.where(first, left, right)
            other_ref[to] = jnp.where(first, right, left)


def blocks_kernel(*refs):
    conv_refs, col_ref, out_ref = refs[: 2 * STREAMS], refs[2 * STREAMS], refs[-1]
    pairs, width = out_ref.shape[1:]
    column = jnp.transpose(col_ref[0])
    each = width // LANES // STREAMS
    for t in range(0, pairs, 16):
        share = [
            [jnp.broadcast_to(column[t + u : t + u + 8, q : q + 1], (8, LANES)) for q in range(2 * TAPS, 2 * TAPS + REACH)]
            for u in (0, 8)
        ]
        for d in range(width // LANES):
            out = []
            for u in range(2):
                total = 0.0
                for r in range(REACH):
                    at = d % each * (HALO + pairs) + HALO + t + 8 * u - r // 2
                    total = total + share[u][r] * conv_refs[r % 2 * STREAMS + d // each][0, 0, pl.ds(at, 8)]
                out.append(total)
            out_ref[0, pl.ds(t, 16), pl.ds(d * LANES, LANES)] = jnp.concatenate(out, axis=0).astype(BF16)


STREAMS = 3


def blocks(conv, columns, pairs, width, start, stop, before=None):
    rows = conv.shape[0]
    conv = conv.reshape(rows, 2 * STREAMS, -1, LANES)
    part = lambda n: pl.BlockSpec((1, 1) + conv.shape[2:], lambda i: (i + start, n, 0, 0))
    return pl.pallas_call(
        blocks_kernel,
        grid=(stop - start,),
        in_specs=[part(n) for n in range(2 * STREAMS)]
        + [pl.BlockSpec((1,) + columns.shape[1:], lambda i: (i + start, 0, 0))]
        + ([] if before is None else [pl.BlockSpec(memory_space=pl.ANY)]),
        out_specs=pl.BlockSpec((1, pairs, width), lambda i: (i + start, 0, 0)),
        out_shape=jax.ShapeDtypeStruct((rows, pairs, width), BF16),
        input_output_aliases={} if before is None else {2 * STREAMS + 1: 0},
        cost_estimate=pl.CostEstimate(
            flops=9 * (stop - start) * pairs * width,
            bytes_accessed=(stop - start) * (4 * conv.size // rows + 2 * pairs * width),
            transcendentals=0,
        ),
        name="blocks",
    )(*[conv] * (2 * STREAMS), columns, *([] if before is None else [before]))


def main(byte_ids, segment_ids, halo, table, conv_weight, scorer, scores, cotangent):
    rows, pairs, width = cotangent.shape
    vocab = table.shape[0]
    assert rows * 8 <= LANES
    padded = -(-pairs // LANES) * LANES + LANES
    tiles = width // LANES
    whole = lambda shape: pl.BlockSpec(shape, lambda i: (0,) * len(shape))
    return pl.pallas_call(
        main_kernel,
        grid=(rows,),
        in_specs=[
            whole(byte_ids.shape),
            whole(segment_ids.shape),
            pl.BlockSpec(memory_space=pltpu.VMEM),
            whole((vocab, width)),
            whole((TAPS, width)),
            whole((width,)),
            pl.BlockSpec(memory_space=pltpu.VMEM),
            pl.BlockSpec((1, pairs, width), lambda i: (i, 0, 0)),
        ],
        out_specs=[
            pl.BlockSpec((None, 2 * tiles * (HALO + pairs), LANES), lambda i: (i, 0, 0)),
            whole((rows, 16, padded)),
            pl.BlockSpec(memory_space=pltpu.VMEM),
            pl.BlockSpec(memory_space=pltpu.VMEM),
        ],
        out_shape=[
            jax.ShapeDtypeStruct((rows, 2 * tiles * (HALO + pairs), LANES), F32),
            jax.ShapeDtypeStruct((rows, 16, padded), F32),
            jax.ShapeDtypeStruct((vocab + 8, width // 2), F32),
            jax.ShapeDtypeStruct((vocab + 8, width // 2), F32),
        ],
        scratch_shapes=[
            pltpu.VMEM(((SPAN + 2 * REACH * TAPS) * padded // LANES * rows, LANES), F32),
            pltpu.VMEM((rows, 2, padded, vocab), BF16),
            pltpu.VMEM((rows, 16, padded), F32),
            pltpu.VMEM((rows, HALO + pairs, 16), F32),
            pltpu.VMEM((2 * TAPS, rows, padded), F32),
            pltpu.VMEM((2 * TAPS, rows, padded), F32),
            pltpu.VMEM((2, tiles, rows, HALO, LANES), F32),
            pltpu.VMEM((2 * tiles * (HALO + pairs), LANES), F32),
            pltpu.VMEM((2 * tiles * (HALO + pairs), LANES), F32),
            pltpu.VMEM((2 * (TAPS - 1) * (8 + pairs), LANES), F32),
            pltpu.VMEM((2 * (TAPS - 1) * (8 + pairs), LANES), F32),
            pltpu.VMEM((pairs, LANES), F32),
            pltpu.VMEM((rows, 8, padded), F32),
            pltpu.VMEM((rows, 2, 2 * TAPS, padded), F32),
            pltpu.VMEM((TAPS, tiles, 8, LANES), F32),
            pltpu.VMEM((TAPS, 2, vocab, pairs), BF16),
            pltpu.VMEM((TAPS, 2, vocab, pairs), BF16),
            pltpu.VMEM((TAPS * vocab, width), F32),
        ],
        name="main",
    )(byte_ids, segment_ids, halo, table, conv_weight, scorer, scores, cotangent)


def add_parts(mine, other, rows_axis, seq_axis, vocab):
    ranks, parts = lax.axis_size(rows_axis), lax.axis_size(seq_axis)
    rank, part = lax.axis_index(rows_axis), lax.axis_index(seq_axis)
    share = vocab // parts

    def swap(x, stride):
        return lax.ppermute(x, rows_axis, [(i, i ^ stride) for i in range(ranks)])

    mine = mine + swap(other, 1)
    rest = mine[vocab:]
    piece = lambda n: jnp.concatenate(
        [lax.dynamic_slice_in_dim(mine, (part + n) % parts * share, share, 0), rest], axis=0
    )
    total = piece(0)
    for n in range(1, parts):
        total = total + lax.ppermute(piece(n), seq_axis, [(i, (i + n) % parts) for i in range(parts)])
    stride = 2
    while stride < ranks:
        total = total + swap(total, stride)
        stride *= 2
    other = swap(total, 1)
    whole = jnp.where(
        rank % 2 == 0, jnp.concatenate([total, other], axis=1), jnp.concatenate([other, total], axis=1)
    )
    return whole[:share], whole[share : share + TAPS], whole[share + TAPS]


def per_device(byte_ids, segment_ids, table, conv_weight, scorer, cotangent):
    parts = lax.axis_size("seq")
    vocab = table.shape[0]
    rows, pairs, width = cotangent.shape
    tail = byte_ids[:, -LANES:] + vocab * segment_ids[:, -LANES:]
    halo = lax.ppermute(tail, "seq", [(i, i + 1) for i in range(parts - 1)])
    scores = score_table(table, conv_weight, scorer)
    conv, columns, mine, other = main(
        byte_ids, segment_ids, halo, table, conv_weight, scorer, scores, cotangent
    )
    cuts = (0, rows * 3 // 8, rows * 5 // 8, rows)
    out = None
    for n in range(3):
        out = blocks(conv, columns, pairs, width, cuts[n], cuts[n + 1], out)
    table_grad, conv_grad, scorer_grad = add_parts(mine, other, "rows", "seq", vocab)
    return (out, table_grad, conv_grad, scorer_grad)


def solution(mesh):
    return jax.shard_map(
        per_device,
        mesh=mesh,
        in_specs=(P("rows", "seq"), P("rows", "seq"), P(), P(), P(), P("rows", "seq", None)),
        out_specs=(P("rows", "seq", None), P("seq", None), P(), P()),
        check_vma=False,
    )
```

```python
import functools

import jax
import jax.numpy as jnp
from jax import lax
from jax.experimental import pallas as pl
from jax.experimental.pallas import tpu as pltpu
from jax.sharding import PartitionSpec as P


TAPS = 4
REACH = 5
SPAN = 8
LANES = 128
F32 = jnp.float32
BF16 = jnp.bfloat16
NT = (((1,), (1,)), ((), ()))


def split(x):
    hi = x.astype(BF16)
    return hi, (x - hi.astype(F32)).astype(BF16)


def dot(a, b):
    return jnp.dot(a, b, preferred_element_type=F32)


def dot_nt(a, b):
    return lax.dot_general(a, b, NT, preferred_element_type=F32)


def lanes_of(width):
    step = min(width, LANES)
    return [pl.ds(at, step) for at in range(0, width, step)]


def look_up(rows_of, index):
    parts = []
    for at in range(0, index.shape[1], LANES):
        part = index[:, at : at + LANES]
        low = part & (LANES - 1)
        take = lambda h: jnp.take_along_axis(
            jnp.broadcast_to(rows_of[h], part.shape), low, axis=1, mode="promise_in_bounds"
        )
        parts.append(jnp.where(part < LANES, take(0), take(1)))
    return jnp.concatenate(parts, axis=1)


HALO = 16
UNITS = 1
GROUPS = 1


def main_kernel(
    byte_ref, seg_ref, halo_ref, table_ref, weight_ref, scorer_ref, cot_ref,
    conv_ref, col_ref, mine_ref, other_ref,
    line_scr, hot_scr, col_scr, column_scr, keep_scr, prob_scr, rim_scr, emb_a, emb_b, mask_a, mask_b, dcol_scr, prod_scr, zeta_scr,
    weight_scr, mix_a, mix_b, sum_scr,
):
    rows, _, padded = col_scr.shape
    vocab, width = table_ref.shape
    pairs = cot_ref.shape[1]
    row = pl.program_id(0)
    tiles = width // LANES

    def back(x, n):
        return pltpu.roll(x, n % padded, axis=1) if n % padded else x

    def keeps(parity, k):
        return keep_scr[parity * TAPS + k] if k else 1.0

    def same(r, k):
        return back(keep_scr[r % 2 * TAPS + k], r // 2) if k else 1.0

    def counts(start):
        total, inverse = 1.0, [1.0]
        for b in range(1, TAPS):
            total = total + keeps(start, b)
            inverse.append(1.0 / total)
        return inverse

    def put(scr, q, value):
        for i in range(rows):
            scr[i, pl.ds(q, 1)] = value[i : i + 1]

    def line(q, tile, i):
        return (q * (padded // LANES) + tile) * rows + i

    def lay(q, value):
        for tile in range(padded // LANES):
            line_scr[pl.ds(line(q, tile, 0), rows)] = value[:, tile * LANES : (tile + 1) * LANES]

    @pl.when(row == 0)
    def _():
        halo = jnp.where(lax.axis_index("seq") == 0, -vocab, halo_ref[...])
        codes = jnp.concatenate(
            [
                jnp.concatenate([halo & (vocab - 1), byte_ref[...]], axis=1),
                jnp.concatenate([halo >> (vocab.bit_length() - 1), seg_ref[...]], axis=1),
            ],
            axis=0,
        )
        codes = codes.astype(F32).astype(BF16)
        reach = codes.shape[1]
        ahead = reach - 2 * pairs
        at = lax.broadcasted_iota(jnp.int32, (reach, padded), 0) - ahead
        lane = lax.broadcasted_iota(jnp.int32, (reach, padded), 1)
        place = at - 2 * jnp.where(lane < pairs, lane, lane - padded)
        byte, seg = [], []
        for parity in range(2):
            found = dot(codes, jnp.where(place == 1 - parity, 1.0, 0.0).astype(BF16))
            byte.append(found[:rows])
            seg.append(found[rows:])
        for parity in range(2):
            put(col_scr, parity, byte[parity])
            for k in range(1, TAPS):
                s = parity + k
                keep = jnp.where(seg[parity] == back(seg[s % 2], s // 2), 1.0, 0.0)
                keep_scr[parity * TAPS + k] = keep
                put(col_scr, 2 + parity * (TAPS - 1) + k - 1, keep)
        bytes_at = [back(byte[s % 2], s // 2) for s in range(SPAN)]
        byte = [b.astype(jnp.int32) for b in byte]
        for s in range(SPAN):
            lay(s, bytes_at[s])
        found = []
        hi, lo = split(weight_ref[...].astype(F32) * scorer_ref[...].reshape(1, -1).astype(F32))
        scores = dot_nt(hi, table_ref[...]) + dot_nt(lo, table_ref[...])
        for k in range(TAPS):
            halves = [scores[k : k + 1, h * LANES : (h + 1) * LANES] for h in range(2)]
            found.append([look_up(halves, byte[parity]) for parity in range(2)])
        scored = [
            sum(keeps(parity, k) * back(found[k][(parity + k) % 2], (parity + k) // 2) for k in range(TAPS))
            for parity in range(2)
        ]
        beta = [0.0] * REACH
        for start in range(2):
            inverse = counts(start)
            running, level = 0.0, []
            for b in range(TAPS):
                running = running + keeps(start, b) * back(scored[(start + b) % 2], (start + b) // 2)
                level.append(running * inverse[b])
            top = functools.reduce(jnp.maximum, level)
            level = [jnp.exp(x - top) for x in level]
            norm = 1.0 / sum(level)
            level = [x * norm for x in level]
            share = 0.0
            for b in range(TAPS - 1, -1, -1):
                prob_scr[start * TAPS + b] = level[b]
                share = share + level[b] * inverse[b]
                beta[start + b] = beta[start + b] + 0.5 * keeps(start, b) * share
        alike = {
            (s, u): bytes_at[s] == bytes_at[u] for s in range(SPAN) for u in range(s + 1, min(s + REACH, SPAN))
        }
        for r in range(REACH):
            put(col_scr, 2 * TAPS + r, beta[r])
        for k in range(TAPS):
            alone = [beta[r] * same(r, k) for r in range(REACH)]
            for r in range(REACH):
                total = alone[r]
                for u in range(REACH):
                    if u != r:
                        total = total + jnp.where(alike[min(r, u) + k, max(r, u) + k], alone[u], 0.0)
                hi = total.astype(BF16).astype(F32)
                lay(SPAN + 2 * (r * TAPS + k), hi)
                lay(SPAN + 2 * (r * TAPS + k) + 1, total - hi)

    deep = HALO + pairs
    group = pairs // GROUPS
    part_v = vocab // GROUPS

    embs, masks, mixes = (emb_a, emb_b), (mask_a, mask_b), (mix_a, mix_b)

    def spot(parity, d):
        return (parity * tiles + d) * deep

    def embed(i, slot, j):
        at = pl.multiple_of(HALO + j * group, 8)
        column = column_scr[i, pl.ds(at, group)]
        value = lax.broadcasted_iota(jnp.int32, (group, vocab), 1).astype(F32)
        hot = [jnp.where(column[:, p : p + 1] == value, 1.0, 0.0).astype(BF16) for p in range(2)]
        for p in range(2):
            hot_scr[i, p, pl.ds(j * group, group)] = hot[p]
        found = dot(jnp.concatenate(hot, axis=0), table_ref[...])
        for p in range(2):
            for d in range(tiles):
                to = pl.multiple_of(spot(p, d) + at, 8)
                embs[slot][pl.ds(to, group)] = found[p * group : (p + 1) * group, d * LANES : (d + 1) * LANES]

    def embed_rim(i, slot):
        for p in range(2):
            for d in range(tiles):
                to = pl.multiple_of(spot(p, d), 8)
                embs[slot][pl.ds(to, HALO)] = rim_scr[p, d, i]

    def mixing(i, slot, j):
        deep_v = 32
        for tile, lane in enumerate(lanes_of(pairs)):
            size = lane.size

            def full(q):
                return jnp.broadcast_to(line_scr[pl.ds(line(q, tile, i), 1)][:, :size], (deep_v, size)).astype(BF16)

            byte = [full(s) for s in range(SPAN)]
            base = lax.broadcasted_iota(jnp.int32, (deep_v, size), 0).astype(F32).astype(BF16)
            for v in range(0, part_v, deep_v):
                value = base + (j * part_v + v)
                hit = [b == value for b in byte]
                at = pl.ds(j * part_v + v, deep_v)
                for k in range(TAPS):
                    for half in range(2):
                        mixed = jnp.zeros((deep_v, size), BF16)
                        for r in range(REACH):
                            mixed = jnp.where(hit[r + k], full(SPAN + 2 * (r * TAPS + k) + half), mixed)
                        mixes[slot][k, half, at, lane] = mixed

    def gather(slot, j, first):
        cot = cot_ref[0]
        at = pl.ds(pl.multiple_of(j * part_v, 16), part_v)
        hi = jnp.concatenate([mixes[slot][k, 0, at] for k in range(TAPS)], axis=0)
        lo = jnp.concatenate([mixes[slot][k, 1, at] for k in range(TAPS)], axis=0)
        if pairs % LANES == 0:
            part = dot(jnp.concatenate([hi, lo], axis=1), jnp.concatenate([cot, cot], axis=0))
        else:
            part = dot(hi, cot) + dot(lo, cot)
        for k in range(TAPS):
            to = pl.ds(pl.multiple_of(k * vocab + j * part_v, 8), part_v)
            more = part[k * part_v : (k + 1) * part_v]
            sum_scr[to] = more if first else sum_scr[to] + more

    def spread(i, slot, at, to, size):
        for t in range(0, size, 8):
            column = column_scr[i, pl.ds(pl.multiple_of(at + t, 8), 8)]
            for q in range(2 * (TAPS - 1)):
                place = pl.multiple_of(q * (8 + pairs) + to + t, 8)
                masks[slot][pl.ds(place, 8)] = jnp.broadcast_to(column[:, 2 + q : 3 + q], (8, LANES))

    def conved(slot, places):
        keep = [
            [masks[slot][pl.ds(pl.multiple_of(q * (8 + pairs) + at - HALO + 8, 8), 8)] for q in range(2 * (TAPS - 1))]
            for at in places
        ]
        for d in range(tiles):
            weight = [weight_scr[k, d] for k in range(TAPS)]
            ready = []
            for n, at in enumerate(places):
                taken = [embs[slot][pl.ds(spot(s % 2, d) + at - s // 2, 8)] for s in range(REACH)]
                for p in range(2):
                    total = weight[0] * taken[p]
                    for k in range(1, TAPS):
                        total = total + keep[n][p * (TAPS - 1) + k - 1] * (weight[k] * taken[p + k])
                    ready.append((p, at, total))
            for p, at, total in ready:
                conv_ref[pl.ds(pl.multiple_of(spot(p, d) + at, 8), 8)] = total

    lane_at = lax.broadcasted_iota(jnp.int32, (8, LANES), 1) - 8 * row

    def convolve(slot, j):
        for t in range(0, group, 8 * UNITS):
            conved(slot, [pl.multiple_of(HALO + j * group + t + 8 * u, 8) for u in range(UNITS)])

    def products(j):
        for t in range(0, group, 16):
            start = pl.multiple_of(j * group + t, 16)
            total = [[0.0] * REACH for _ in range(2)]
            for d in range(tiles):
                grad = cot_ref[0, pl.ds(start, 16), pl.ds(d * LANES, LANES)].astype(F32)
                for u in range(2):
                    at = HALO + start + 8 * u
                    for r in range(REACH):
                        conv = conv_ref[pl.ds(spot(r % 2, d) + at - r // 2, 8)]
                        total[u][r] = total[u][r] + grad[8 * u : 8 * u + 8] * conv
            for u in range(2):
                to = pl.ds(pl.multiple_of(start + 8 * u, 8), 8)
                found = dcol_scr[to]
                for r in range(REACH):
                    found = jnp.where(lane_at == r, jnp.sum(total[u][r], axis=1, keepdims=True), found)
                dcol_scr[to] = found

    @pl.when(row == 0)
    def _():
        for i in range(rows):
            column = jnp.transpose(col_scr[i])
            column_scr[i, pl.ds(0, HALO)] = column[padded - HALO :]
            column_scr[i, pl.ds(HALO, pairs)] = column[:pairs]
        value = lax.broadcasted_iota(jnp.int32, (HALO, vocab), 1).astype(F32)
        for p in range(2):
            hot = [
                jnp.where(column_scr[i, pl.ds(0, HALO)][:, p : p + 1] == value, 1.0, 0.0).astype(BF16)
                for i in range(rows)
            ]
            for i in range(rows):
                hot_scr[i, p, pl.ds(pairs, padded - HALO - pairs)] = jnp.zeros((padded - HALO - pairs, vocab), BF16)
                hot_scr[i, p, pl.ds(padded - HALO, HALO)] = hot[i]
            found = dot(jnp.concatenate(hot, axis=0), table_ref[...])
            for d in range(tiles):
                for i in range(rows):
                    rim_scr[p, d, i] = found[i * HALO : (i + 1) * HALO, d * LANES : (d + 1) * LANES]
        for k in range(TAPS):
            for d in range(tiles):
                lanes = pl.ds(d * LANES, LANES)
                weight_scr[k, d] = jnp.broadcast_to(weight_ref[k : k + 1, lanes].astype(F32), (8, LANES))
        dcol_scr[...] = jnp.zeros_like(dcol_scr)
        embed_rim(0, 0)
        spread(0, 0, HALO - 8, 0, 8)
        col_ref[...] = col_scr[...]

        @pl.loop(0, GROUPS)
        def _(j):
            spread(0, 0, HALO + j * group, 8 + j * group, group)
            embed(0, 0, j)
            mixing(0, 0, j)

    def work(slot, more, first=False):
        if more:
            embed_rim(row + 1, 1 - slot)
            spread(row + 1, 1 - slot, HALO - 8, 0, 8)
        conved(slot, [HALO - 8])

        @pl.loop(0, GROUPS)
        def _(j):
            convolve(slot, j)
            gather(slot, j, first)
            if more:
                spread(row + 1, 1 - slot, HALO + j * group, 8 + j * group, group)
                mixing(row + 1, 1 - slot, j)
                embed(row + 1, 1 - slot, j)
            products(j)

    last = rows - 1
    pl.when(row == 0)(lambda: work(0, last > 0, True))
    pl.when((row > 0) & (row < last) & (row % 2 == 0))(lambda: work(0, True))
    pl.when((row < last) & (row % 2 == 1))(lambda: work(1, True))
    pl.when((row > 0) & (row == last))(lambda: work(last % 2, False))

    @pl.when(row == rows - 1)
    def _():
        inside = lax.broadcasted_iota(jnp.int32, (rows, padded), 1) < pairs
        turned = jnp.transpose(dcol_scr[...])
        for i in range(rows):
            prod_scr[i, :, pl.ds(0, pairs)] = turned[8 * i : 8 * i + 8]
        products = [prod_scr[:, r] for r in range(REACH)]
        eta = [0.0] * REACH
        for start in range(2):
            inverse = counts(start)
            prob = [prob_scr[start * TAPS + b] for b in range(TAPS)]
            running, grad = 0.0, []
            for b in range(TAPS):
                running = running + keeps(start, b) * products[start + b]
                grad.append(0.5 * running * inverse[b])
            mean = sum(p * g for p, g in zip(prob, grad))
            share = 0.0
            for b in range(TAPS - 1, -1, -1):
                share = share + prob[b] * (grad[b] - mean) * inverse[b]
                eta[start + b] = eta[start + b] + keeps(start, b) * share
        eta = [jnp.where(inside, x, 0.0) for x in eta]
        alpha = [sum(back(eta[r], -(r // 2)) for r in range(parity, REACH, 2)) for parity in range(2)]
        for parity in range(2):
            for k in range(TAPS):
                other = (parity + k) % 2
                ahead = (k + 1 - parity) // 2
                hi = back(alpha[other] * keeps(other, k), -ahead)
                low = hi - hi.astype(BF16).astype(F32)
                hi = hi - low
                for i in range(rows):
                    zeta_scr[i, parity, k : k + 1] = hi[i : i + 1]
                    zeta_scr[i, parity, TAPS + k : TAPS + k + 1] = low[i : i + 1]
        found = jnp.zeros((2 * TAPS, vocab), F32)
        for i in range(rows):
            for p in range(2):
                found = found + dot(zeta_scr[i, p].astype(BF16), hot_scr[i, p])
        found = found[:TAPS] + found[TAPS:]
        scorer = scorer_ref[...].reshape(1, -1).astype(F32)
        weight = weight_ref[...].astype(F32)
        table = table_ref[...].astype(F32)
        hi, lo = split(found)
        sums = dot(hi, table_ref[...]) + dot(lo, table_ref[...])
        hi, lo = hi.astype(F32), lo.astype(F32)
        near, rest = split(weight * scorer)
        near, rest = near.astype(F32), rest.astype(F32)
        grad = lax.dot_general(
            jnp.concatenate([hi, lo, hi], axis=0).astype(BF16),
            jnp.concatenate([near, near, rest], axis=0).astype(BF16),
            (((0,), (0,)), ((), ())),
            preferred_element_type=F32,
        )
        conv, score_grad = [], 0.0
        for k in range(TAPS):
            total = sum_scr[pl.ds(k * vocab, vocab)]
            grad = grad + weight[k : k + 1] * total
            conv.append(jnp.sum(table * total, axis=0, keepdims=True) + scorer * sums[k : k + 1])
            score_grad = score_grad + weight[k : k + 1] * sums[k : k + 1]
        rest = jnp.concatenate(conv + [score_grad, jnp.zeros((8 - TAPS - 1, width), F32)], axis=0)
        half = width // 2
        first = lax.axis_index("rows") % 2 == 0
        for at, value in ((0, grad), (vocab, rest)):
            to = pl.ds(at, value.shape[0])
            left, right = value[:, :half], value[:, half:]
            mine_ref[to] = jnp.where(first, left, right)
            other_ref[to] = jnp.where(first, right, left)


def blocks_kernel(*refs):
    conv_refs, col_ref, out_ref = refs[: 2 * STREAMS], refs[2 * STREAMS], refs[-1]
    pairs, width = out_ref.shape[1:]
    column = jnp.transpose(col_ref[0])
    each = width // LANES // STREAMS
    for t in range(0, pairs, 16):
        share = [
            [jnp.broadcast_to(column[t + u : t + u + 8, q : q + 1], (8, LANES)) for q in range(2 * TAPS, 2 * TAPS + REACH)]
            for u in (0, 8)
        ]
        for d in range(width // LANES):
            out = []
            for u in range(2):
                total = 0.0
                for r in range(REACH):
                    at = d % each * (HALO + pairs) + HALO + t + 8 * u - r // 2
                    total = total + share[u][r] * conv_refs[r % 2 * STREAMS + d // each][0, 0, pl.ds(at, 8)]
                out.append(total)
            out_ref[0, pl.ds(t, 16), pl.ds(d * LANES, LANES)] = jnp.concatenate(out, axis=0).astype(BF16)


STREAMS = 3


def blocks(conv, columns, pairs, width, start, stop, before=None):
    rows = conv.shape[0]
    conv = conv.reshape(rows, 2 * STREAMS, -1, LANES)
    part = lambda n: pl.BlockSpec((1, 1) + conv.shape[2:], lambda i: (i + start, n, 0, 0))
    return pl.pallas_call(
        blocks_kernel,
        grid=(stop - start,),
        in_specs=[part(n) for n in range(2 * STREAMS)]
        + [pl.BlockSpec((1,) + columns.shape[1:], lambda i: (i + start, 0, 0))]
        + ([] if before is None else [pl.BlockSpec(memory_space=pl.ANY)]),
        out_specs=pl.BlockSpec((1, pairs, width), lambda i: (i + start, 0, 0)),
        out_shape=jax.ShapeDtypeStruct((rows, pairs, width), BF16),
        input_output_aliases={} if before is None else {2 * STREAMS + 1: 0},
        cost_estimate=pl.CostEstimate(
            flops=9 * (stop - start) * pairs * width,
            bytes_accessed=(stop - start) * (4 * conv.size // rows + 2 * pairs * width),
            transcendentals=0,
        ),
        name="blocks",
    )(*[conv] * (2 * STREAMS), columns, *([] if before is None else [before]))


def main(byte_ids, segment_ids, halo, table, conv_weight, scorer, cotangent):
    rows, pairs, width = cotangent.shape
    vocab = table.shape[0]
    assert rows * 8 <= LANES
    padded = -(-pairs // LANES) * LANES + LANES
    tiles = width // LANES
    whole = lambda shape: pl.BlockSpec(shape, lambda i: (0,) * len(shape))
    return pl.pallas_call(
        main_kernel,
        grid=(rows,),
        in_specs=[
            whole(byte_ids.shape),
            whole(segment_ids.shape),
            pl.BlockSpec(memory_space=pltpu.VMEM),
            whole((vocab, width)),
            whole((TAPS, width)),
            whole((width,)),
            pl.BlockSpec((1, pairs, width), lambda i: (i, 0, 0)),
        ],
        out_specs=[
            pl.BlockSpec((None, 2 * tiles * (HALO + pairs), LANES), lambda i: (i, 0, 0)),
            whole((rows, 16, padded)),
            pl.BlockSpec(memory_space=pltpu.VMEM),
            pl.BlockSpec(memory_space=pltpu.VMEM),
        ],
        out_shape=[
            jax.ShapeDtypeStruct((rows, 2 * tiles * (HALO + pairs), LANES), F32),
            jax.ShapeDtypeStruct((rows, 16, padded), F32),
            jax.ShapeDtypeStruct((vocab + 8, width // 2), F32),
            jax.ShapeDtypeStruct((vocab + 8, width // 2), F32),
        ],
        scratch_shapes=[
            pltpu.VMEM(((SPAN + 2 * REACH * TAPS) * padded // LANES * rows, LANES), F32),
            pltpu.VMEM((rows, 2, padded, vocab), BF16),
            pltpu.VMEM((rows, 16, padded), F32),
            pltpu.VMEM((rows, HALO + pairs, 16), F32),
            pltpu.VMEM((2 * TAPS, rows, padded), F32),
            pltpu.VMEM((2 * TAPS, rows, padded), F32),
            pltpu.VMEM((2, tiles, rows, HALO, LANES), F32),
            pltpu.VMEM((2 * tiles * (HALO + pairs), LANES), F32),
            pltpu.VMEM((2 * tiles * (HALO + pairs), LANES), F32),
            pltpu.VMEM((2 * (TAPS - 1) * (8 + pairs), LANES), F32),
            pltpu.VMEM((2 * (TAPS - 1) * (8 + pairs), LANES), F32),
            pltpu.VMEM((pairs, LANES), F32),
            pltpu.VMEM((rows, 8, padded), F32),
            pltpu.VMEM((rows, 2, 2 * TAPS, padded), F32),
            pltpu.VMEM((TAPS, tiles, 8, LANES), F32),
            pltpu.VMEM((TAPS, 2, vocab, pairs), BF16),
            pltpu.VMEM((TAPS, 2, vocab, pairs), BF16),
            pltpu.VMEM((TAPS * vocab, width), F32),
        ],
        name="main",
    )(byte_ids, segment_ids, halo, table, conv_weight, scorer, cotangent)


def add_parts(mine, other, rows_axis, seq_axis, vocab):
    ranks, parts = lax.axis_size(rows_axis), lax.axis_size(seq_axis)
    rank, part = lax.axis_index(rows_axis), lax.axis_index(seq_axis)
    share = vocab // parts

    def swap(x, stride):
        return lax.ppermute(x, rows_axis, [(i, i ^ stride) for i in range(ranks)])

    mine = mine + swap(other, 1)
    rest = mine[vocab:]
    piece = lambda n: jnp.concatenate(
        [lax.dynamic_slice_in_dim(mine, (part + n) % parts * share, share, 0), rest], axis=0
    )
    total = piece(0)
    for n in range(1, parts):
        total = total + lax.ppermute(piece(n), seq_axis, [(i, (i + n) % parts) for i in range(parts)])
    stride = 2
    while stride < ranks:
        total = total + swap(total, stride)
        stride *= 2
    other = swap(total, 1)
    whole = jnp.where(
        rank % 2 == 0, jnp.concatenate([total, other], axis=1), jnp.concatenate([other, total], axis=1)
    )
    return whole[:share], whole[share : share + TAPS], whole[share + TAPS]


def per_device(byte_ids, segment_ids, table, conv_weight, scorer, cotangent):
    parts = lax.axis_size("seq")
    vocab = table.shape[0]
    rows, pairs, width = cotangent.shape
    tail = byte_ids[:, -LANES:] + vocab * segment_ids[:, -LANES:]
    halo = lax.ppermute(tail, "seq", [(i, i + 1) for i in range(parts - 1)])
    conv, columns, mine, other = main(
        byte_ids, segment_ids, halo, table, conv_weight, scorer, cotangent
    )
    cuts = (0, rows // 8, rows * 3 // 8, rows * 5 // 8, rows)
    out = None
    for n in range(4):
        out = blocks(conv, columns, pairs, width, cuts[n], cuts[n + 1], out)
    table_grad, conv_grad, scorer_grad = add_parts(mine, other, "rows", "seq", vocab)
    return (out, table_grad, conv_grad, scorer_grad)


def solution(mesh):
    return jax.shard_map(
        per_device,
        mesh=mesh,
        in_specs=(P("rows", "seq"), P("rows", "seq"), P(), P(), P(), P("rows", "seq", None)),
        out_specs=(P("rows", "seq", None), P("seq", None), P(), P()),
        check_vma=False,
    )
```
